512 devices in a mesh: face: 16 (over x, z_hi, core), patch: 32 (over z_lo, y).
Axes of the slice: x: 4, y: 8, z: 8 (z_hi: 2, z_lo: 4; z = z_hi * 4 + z_lo), core: 2. Of those that a mesh axis runs over, the one named last changes fastest.
Arguments:
- dust_map: float32 [128, 32768], P('face', 'patch'), may hold values from -12 to 12
- seam_flags: int32 [16, 32, 4], P('face', 'patch'), may hold values from 0 to 1
- block_weights: int32 [128, 4096], P('face', 'patch'), may hold values from 1 to 4
Outputs:
- energy_field: float32 [128, 32768], P('face', 'patch')
- face_moments: float32 [16, 3, 128], P('face')
- sky_moments: float32 [3, 128], replicated
The draws below stay inside these ranges and needn't reach their ends.
All inputs are finite; a program needn't handle non-finite values.
Results may differ from the reference program's by a relative error of at most 0.0003.
Values sent between devices are 32-bit elements; how exact they have to be, the bound alone decides.
No kernel may reach another device: no remote copies, remote signals or barrier semaphores. Data moves between devices by JAX's collectives and lax.ppermute only.
A program may use at most 64 MiB of HBM per device.

```python
import math
import jax
import jax.numpy as jnp
import numpy as np
from jax import lax

TILE_ROWS = 8
TILE_COLS = 1024
BLOCK_COLS = 8
ROWS = 128
COLS = 32768
N_FACE = 16
N_PATCH = 32


def draw_dust_map(key, part):
    noise_key, rough_key = jax.random.split(key)
    row_pos = lax.broadcasted_iota(jnp.float32, (ROWS, COLS), 0) / ROWS
    col_pos = lax.broadcasted_iota(jnp.float32, (ROWS, COLS), 1) / COLS
    amplitude = jnp.exp(0.5 * math.log(3.0) * (row_pos + col_pos))
    roughness = jnp.exp(jax.random.uniform(rough_key, (ROWS, COLS), jnp.float32, -0.35, 0.35))
    noise_part = jax.random.truncated_normal(noise_key, -4.0, 4.0, (ROWS, COLS), jnp.float32)
    sampled = amplitude * roughness * noise_part
    return jnp.clip(sampled, -12.0, 12.0)


def set_ends(values, stream_key, smallest, high):
    dims = values.shape
    place = [jax.random.randint(jax.random.fold_in(stream_key, axis), (), 0, dims[axis]) for axis in range(len(dims))]
    values = values.at[tuple(place)].set(smallest)
    longest = dims.index(max(dims))
    place[longest] = (place[longest] + 1) % dims[longest]
    return values.at[tuple(place)].set(high)


def setup_inputs(seed: int = 0) -> dict:
    keys = jax.random.split(jax.random.key(seed), 4)
    return {
        "dust_map": draw_dust_map(jax.random.fold_in(keys[3], 71), 0),
        "seam_flags": set_ends(jax.random.randint(keys[1], (N_FACE, N_PATCH, 4), 0, 2), jax.random.fold_in(keys[1], 1), 0, 1).astype(jnp.int32),
        "block_weights": set_ends(jax.random.randint(keys[2], (ROWS, COLS // BLOCK_COLS), 1, 5), jax.random.fold_in(keys[2], 1), 1, 4).astype(jnp.int32),
    }


rim_depth = 4
epsilon = 1e-06
pair_list = ((0, 1), (0, 2), (1, 2))

def filter_table():
    shift_rows = np.repeat(np.array([-1.0, 0.0, 1.0]), 3)
    shift_cols = np.tile(np.array([-1.0, 0.0, 1.0]), 3)
    envelope = np.exp(-(shift_rows ** 2 + shift_cols ** 2) / 1.28)
    real_rows = []
    imag_rows = []
    for orient in range(8):
        heading = math.pi * orient / 8.0
        phases = 2.2 * (shift_rows * math.cos(heading) + shift_cols * math.sin(heading))
        cosine_part = np.cos(phases) - np.sum(envelope * np.cos(phases)) / np.sum(envelope)
        sine_part = np.sin(phases) - np.sum(envelope * np.sin(phases)) / np.sum(envelope)
        norm_sq = np.sum(envelope ** 2 * (cosine_part ** 2 + sine_part ** 2))
        real_rows.append(envelope * cosine_part / np.sqrt(norm_sq))
        imag_rows.append(envelope * sine_part / np.sqrt(norm_sq))
    return np.stack(real_rows + imag_rows).astype(np.float32)

def turn_rims(extended, seam_bits):
    margin = rim_depth
    top_rim = extended[..., :margin, margin:-margin]
    bottom_rim = extended[..., -margin:, margin:-margin]
    left_rim = extended[..., margin:-margin, :margin]
    right_rim = extended[..., margin:-margin, -margin:]
    top_rim = jnp.where(seam_bits[0] > 0, jnp.flip(top_rim, -1), top_rim)
    bottom_rim = jnp.where(seam_bits[1] > 0, jnp.flip(bottom_rim, -1), bottom_rim)
    left_rim = jnp.where(seam_bits[2] > 0, jnp.flip(left_rim, -2), left_rim)
    right_rim = jnp.where(seam_bits[3] > 0, jnp.flip(right_rim, -2), right_rim)
    upper_band = jnp.concatenate([extended[..., :margin, :margin], top_rim, extended[..., :margin, -margin:]], axis=-1)
    middle_band = jnp.concatenate([left_rim, extended[..., margin:-margin, margin:-margin], right_rim], axis=-1)
    lower_band = jnp.concatenate([extended[..., -margin:, :margin], bottom_rim, extended[..., -margin:, -margin:]], axis=-1)
    return jnp.concatenate([upper_band, middle_band, lower_band], axis=-2)

def stencil(extended, dilation, tile_rows, tile_cols, filters):
    pieces = []
    for shift_row in (-1, 0, 1):
        for shift_col in (-1, 0, 1):
            first_row = rim_depth + shift_row * dilation
            first_col = rim_depth + shift_col * dilation
            pieces.append(extended[..., first_row:first_row + tile_rows, first_col:first_col + tile_cols])
    stacked = jnp.stack(pieces, 0)
    return jnp.einsum('kt,t...->k...', filters, stacked, precision=lax.Precision.HIGHEST)

def first_layer(extended, tile_rows, tile_cols, filters):
    responses = jnp.stack([stencil(extended, 2 ** octave, tile_rows, tile_cols, filters) for octave in range(3)])
    moduli = jnp.sqrt(responses[:, :8] ** 2 + responses[:, 8:] ** 2 + epsilon)
    return (responses, moduli)

def second_layer(rimmed, responses, weights, scales, filters, tile_rows, tile_cols):
    moment_rows = []
    energy_parts = []
    for fine_level, coarse_level in pair_list:
        outputs = stencil(rimmed[8 * fine_level:8 * fine_level + 8], 2 ** coarse_level, tile_rows, tile_cols, filters)
        outputs = outputs.reshape(2, 8, 8, tile_rows, tile_cols)
        coarse = (responses[coarse_level] * scales[coarse_level]).reshape(2, 8, tile_rows, tile_cols)
        squares = outputs * outputs
        third_order = jnp.einsum('atrc,atsrc->st', coarse * weights, outputs, precision=lax.Precision.HIGHEST)
        fourth_order = jnp.einsum('atsrc,rc->st', squares, weights, precision=lax.Precision.HIGHEST)
        moment_rows.append(jnp.concatenate([third_order.reshape(64), fourth_order.reshape(64)]))
        energy_parts.append(lax.optimization_barrier(jnp.sum(squares, axis=(0, 1, 2))))
    return (jnp.stack(moment_rows), jnp.stack(energy_parts))

def reference(dust_map, seam_flags, block_weights):
    filters = jnp.asarray(filter_table())
    tile_rows = TILE_ROWS
    tile_cols = TILE_COLS
    repeat_by = dust_map.shape[1] // block_weights.shape[1]
    weights_all = jnp.repeat(block_weights.astype(jnp.float32), repeat_by, axis=1)
    padded = jnp.pad(dust_map, rim_depth, mode='wrap')
    columns_all = jnp.arange(N_PATCH, dtype=jnp.int32)

    def row_weights(face_row):
        band_rows = lax.dynamic_slice_in_dim(weights_all, face_row * tile_rows, tile_rows, 0)
        return band_rows.reshape(tile_rows, N_PATCH, tile_cols).transpose(1, 0, 2)

    def row_first(face_row):
        band_rows = lax.dynamic_slice_in_dim(padded, face_row * tile_rows, tile_rows + 2 * rim_depth, 0)
        windows = jax.vmap(lambda column: lax.dynamic_slice_in_dim(band_rows, column * tile_cols, tile_cols + 2 * rim_depth, 1))(columns_all)
        windows = jax.vmap(turn_rims)(windows, seam_flags[face_row])
        return jax.vmap(lambda window: first_layer(window, tile_rows, tile_cols, filters))(windows)

    def row_power(face_row):
        moduli = row_first(face_row)[1]
        weights = row_weights(face_row)
        terms = jnp.einsum('pjtrc,prc->j', moduli * moduli, weights, precision=lax.Precision.HIGHEST)
        return (terms, jnp.sum(weights))
    face_power, face_weight = lax.map(row_power, jnp.arange(N_FACE, dtype=jnp.int32))
    weight_sum = jnp.sum(face_weight)
    levels = lax.optimization_barrier(jnp.sum(face_power, 0)) / (8.0 * weight_sum)
    scales = 1.0 / jnp.sqrt(levels)

    def strip_of(moduli):
        fields = moduli[:, :2] * scales[None, :2, None, None, None]
        fields = fields.reshape(N_PATCH, 16, tile_rows, tile_cols)
        return fields.transpose(1, 2, 0, 3).reshape(16, tile_rows, N_PATCH * tile_cols)

    def row_second(face_row):
        responses, moduli = row_first(face_row)
        above = strip_of(row_first((face_row + N_FACE - 1) % N_FACE)[1])
        below = strip_of(row_first((face_row + 1) % N_FACE)[1])
        strips = jnp.concatenate([above, strip_of(moduli), below], axis=1)
        band_rows = strips[:, tile_rows - rim_depth:2 * tile_rows + rim_depth]
        band_rows = jnp.pad(band_rows, ((0, 0), (0, 0), (rim_depth, rim_depth)), mode='wrap')
        windows = jax.vmap(lambda column: lax.dynamic_slice_in_dim(band_rows, column * tile_cols, tile_cols + 2 * rim_depth, 2))(columns_all)
        windows = jax.vmap(turn_rims)(windows, seam_flags[face_row])
        weights = row_weights(face_row)

        def one_tile(inputs):
            return second_layer(inputs[0], inputs[1], inputs[2], scales, filters, tile_rows, tile_cols)
        moment_rows, energy_parts = lax.map(one_tile, (windows, responses, weights))
        energy = lax.optimization_barrier(jnp.sum(energy_parts, 1)) / 192.0
        return (lax.optimization_barrier(jnp.sum(moment_rows, 0)), energy.transpose(1, 0, 2).reshape(tile_rows, N_PATCH * tile_cols))
    face_raw, energy_rows = lax.map(row_second, jnp.arange(N_FACE, dtype=jnp.int32))
    face_moments = face_raw / face_weight[:, None, None]
    sky_moments = lax.optimization_barrier(jnp.sum(face_raw, 0)) / weight_sum
    energy_field = energy_rows.reshape(N_FACE * tile_rows, N_PATCH * tile_cols)
    return (energy_field, face_moments, sky_moments)
```

```python
import math

import jax
import jax.numpy as jnp
import numpy as np
from jax import lax
from jax.experimental import pallas as pl
from jax.experimental.pallas import tpu as pltpu
from jax.sharding import Mesh
from jax.sharding import PartitionSpec as P

EPS = 1e-06
PAIRS = ((0, 1), (0, 2), (1, 2))
FACE = ("x", "zh", "core")
PATCH = ("zl", "y")
FLAG_LANE = 32


def filter_features():
    rows = np.repeat(np.array([-1.0, 0.0, 1.0]), 3)
    cols = np.tile(np.array([-1.0, 0.0, 1.0]), 3)
    env = np.exp(-(rows**2 + cols**2) / 1.28)
    at = {(int(a), int(b)): i for i, (a, b) in enumerate(zip(rows, cols))}
    picks = [at[0, 1], at[1, 0], at[1, 1], at[1, -1]]
    even, odd = [], []
    for t in range(8):
        h = math.pi * t / 8.0
        ph = 2.2 * (rows * math.cos(h) + cols * math.sin(h))
        c = np.cos(ph) - np.sum(env * np.cos(ph)) / np.sum(env)
        s = np.sin(ph) - np.sum(env * np.sin(ph)) / np.sum(env)
        norm = np.sqrt(np.sum(env**2 * (c**2 + s**2)))
        for src, dst in ((env * c / norm, even), (env * s / norm, odd)):
            v = src[picks]
            dst.append([v[0], v[1], (v[2] + v[3]) / 2, (v[2] - v[3]) / 2])
    out = np.array([even, odd])
    out[np.abs(out) < 1e-12] = 0.0
    return out


TABLE = filter_features()


def features(top, mid, bot, left, right):
    tl, tr = left(top), right(top)
    ml, mr = left(mid), right(mid)
    bl, br = left(bot), right(bot)
    top, mid, bot = (v[len(v) // 2] if isinstance(v, tuple) else v for v in (top, mid, bot))
    two = mid + mid
    s1, s2 = br + tl, bl + tr
    d1, d2 = br - tl, bl - tr
    return (
        ml + mr - two,
        top + bot - two,
        s1 + s2 - (two + two),
        s1 - s2,
        mr - ml,
        bot - top,
        d1 + d2,
        d1 - d2,
    )


def combos(ft):
    e01, e10, p, q, o01, o10, po, qo = ft

    def lin(pairs):
        total = None
        for c, v in pairs:
            if c == 0.0:
                continue
            term = float(c) * v
            total = term if total is None else total + term
        return total

    re, im = [None] * 8, [None] * 8
    for t in (0, 4):
        ce, co = TABLE[0, t], TABLE[1, t]
        re[t] = lin(zip(ce, (e01, e10, p, q)))
        im[t] = lin(zip(co, (o01, o10, po, qo)))
    for t in (1, 2, 3):
        ce, co = TABLE[0, t], TABLE[1, t]
        a, b = lin(zip(ce[:3], (e01, e10, p))), lin([(ce[3], q)])
        re[t], re[8 - t] = a + b, a - b
        a = lin([(co[0], o01), (co[3], qo)])
        b = lin([(co[1], o10), (co[2], po)])
        im[t], im[8 - t] = a + b, a - b
    return re, im


def main_kernel(own, above, below, bw, stats, en0, en1, xt, xud, fe, mm, sm, zz, wx, acc, es):
    f32 = jnp.float32
    lane = lax.broadcasted_iota(jnp.int32, (8, 128), 1)
    sub = lax.broadcasted_iota(jnp.int32, (8, 128), 0)
    low = lane < 64
    back_lane, back_row = 127 - lane, 7 - sub

    def revl(v):
        return jnp.take_along_axis(v, back_lane, axis=1, mode="promise_in_bounds")

    def revr(v):
        return jnp.take_along_axis(v, back_row, axis=0, mode="promise_in_bounds")

    def flag(pack, i):
        return jnp.broadcast_to(pack[:, FLAG_LANE + i : FLAG_LANE + i + 1], (8, 128)) > 0.5

    pk = lambda ref, i: ref[:, 1024 + 128 * i : 1152 + 128 * i]
    pt, plf, prt = pk(own, 0), pk(own, 1), pk(own, 2)
    pu, pul, pur = pk(above, 0), pk(above, 1), pk(above, 2)
    pd, pdl, pdr = pk(below, 0), pk(below, 1), pk(below, 2)
    w_ = jnp.where
    turn_t, turn_u, turn_d = revr(pt), revr(pu), revr(pd)
    revl_l, revl_r = revl(plf), revl(prt)
    f0, f1, f2, f3 = (flag(pt, i) for i in range(4))

    grow = lax.broadcasted_iota(jnp.int32, (128, 1024), 1) // 8 == lax.broadcasted_iota(
        jnp.int32, (128, 1024), 0
    )
    wide = jnp.dot(
        bw[...].astype(jnp.bfloat16), grow.astype(jnp.bfloat16), preferred_element_type=f32
    )
    for b in range(8):
        wx[b] = wide[:, 128 * b : 128 * b + 128]

    def blk(b):
        return slice(128 * b, 128 * b + 128)

    f0d, f1u = flag(pd, 0), flag(pu, 1)
    for b in range(8):
        t_b, t_r = own[:, blk(b)], revl(own[:, blk(7 - b)])
        u_b, u_r = above[:, blk(b)], revl(above[:, blk(7 - b)])
        d_b, d_r = below[:, blk(b)], revl(below[:, blk(7 - b)])
        xt[4:12, blk(b + 1)] = t_b
        xt[0:4, blk(b + 1)] = w_(f0, u_r, u_b)[4:8]
        xt[12:16, blk(b + 1)] = w_(f1, d_r, d_b)[0:4]
        xud[0:6, blk(b + 1)] = u_b[2:8]
        xud[6:8, blk(b + 1)] = w_(f1u, t_r, t_b)[0:2]
        xud[8:10, blk(b + 1)] = w_(f0d, t_r, t_b)[6:8]
        xud[10:16, blk(b + 1)] = d_b[0:6]
    xt[4:12, blk(0)] = w_(f2, revr(plf), plf)
    xt[0:4, blk(0)] = pul[4:8]
    xt[12:16, blk(0)] = pdl[0:4]
    xt[4:12, blk(9)] = w_(f3, revr(prt), prt)
    xt[0:4, blk(9)] = pur[4:8]
    xt[12:16, blk(9)] = pdr[0:4]
    xud[0:6, blk(0)] = w_(flag(pu, 2), revr(pul), pul)[2:8]
    xud[6:8, blk(0)] = plf[0:2]
    xud[8:10, blk(0)] = plf[6:8]
    xud[10:16, blk(0)] = w_(flag(pd, 2), revr(pdl), pdl)[0:6]
    xud[0:6, blk(9)] = w_(flag(pu, 3), revr(pur), pur)[2:8]
    xud[6:8, blk(9)] = prt[0:2]
    xud[8:10, blk(9)] = prt[6:8]
    xud[10:16, blk(9)] = w_(flag(pd, 3), revr(pdr), pdr)[0:6]
    xt[4:12, blk(10)] = w_(low, w_(flag(plf, 3), turn_t, pt), plf)
    xt[0:4, blk(10)] = w_(low, pu, w_(flag(plf, 0), revl(pul), pul))[4:8]
    xt[12:16, blk(10)] = w_(low, pd, w_(flag(plf, 1), revl(pdl), pdl))[0:4]
    xt[4:12, blk(11)] = w_(low, prt, w_(flag(prt, 2), turn_t, pt))
    xt[0:4, blk(11)] = w_(low, w_(flag(prt, 0), revl(pur), pur), pu)[4:8]
    xt[12:16, blk(11)] = w_(low, w_(flag(prt, 1), revl(pdr), pdr), pd)[0:4]
    xud[0:6, blk(10)] = w_(low, w_(flag(pul, 3), turn_u, pu), pul)[2:8]
    xud[6:8, blk(10)] = w_(low, pt, w_(flag(pul, 1), revl_l, plf))[0:2]
    xud[8:10, blk(10)] = w_(low, pt, w_(flag(pdl, 0), revl_l, plf))[6:8]
    xud[10:16, blk(10)] = w_(low, w_(flag(pdl, 3), turn_d, pd), pdl)[0:6]
    xud[0:6, blk(11)] = w_(low, pur, w_(flag(pur, 2), turn_u, pu))[2:8]
    xud[6:8, blk(11)] = w_(low, w_(flag(pur, 1), revl_r, prt), pt)[0:2]
    xud[8:10, blk(11)] = w_(low, w_(flag(pdr, 0), revl_r, prt), pt)[6:8]
    xud[10:16, blk(11)] = w_(low, pdr, w_(flag(pdr, 2), turn_d, pd))[0:6]

    def store_features(slot, load, d):
        first, last = lane < d, lane >= 128 - d

        def left(v):
            return pltpu.roll(w_(last, v[0], v[1]), d, 1)

        def right(v):
            return pltpu.roll(w_(first, v[2], v[1]), 128 - d, 1)

        def left1(v):
            return pltpu.roll(v, d, 1)

        def right1(v):
            return pltpu.roll(v, 128 - d, 1)

        for b in range(1, 9):
            rows = [tuple(load(s, c) for c in (b - 1, b, b + 1)) for s in (-d, 0, d)]
            for k, v in enumerate(features(*rows, left, right)):
                fe[slot, k, b] = v
        if d < 4:
            for b, dst in ((10, 0), (11, 9)):
                rows = [load(s, b) for s in (-d, 0, d)]
                for k, v in enumerate(features(*rows, left1, right1)):
                    fe[slot, k, dst] = v

    def load_own(s, b):
        return xt[4 + s : 12 + s, blk(b)]

    def load_ud(s, b):
        return jnp.concatenate([xud[2 + s : 6 + s, blk(b)], xud[10 + s : 14 + s, blk(b)]], 0)

    for j in range(3):
        store_features(j, load_own, 2**j)
    for j in range(2):
        store_features(3 + j, load_ud, 2**j)

    def column(vals):
        out = jnp.full((8, 128), float(vals[0]), f32)
        for t in range(1, 8):
            out = w_(sub == t, float(vals[t]), out)
        return out

    ce = [column(TABLE[0, :, k]) for k in range(4)]
    co = [column(TABLE[1, :, k]) for k in range(4)]

    def spread(ref, *at):
        *lead, r = at
        return ref[(*lead, pl.ds(r, 8, stride=0), slice(None))]

    def response(slot, r, b):
        v = [spread(fe, slot, k, b, r) for k in range(8)]
        re = ce[0] * v[0] + ce[1] * v[1] + (ce[2] * v[2] + ce[3] * v[3])
        im = co[0] * v[4] + co[1] * v[5] + (co[2] * v[6] + co[3] * v[7])
        return re, im, re * re + im * im

    powers = []
    for j in range(3):

        def row(r, total, j=j):
            for b in range(1, 9):
                wr = spread(wx, b - 1, r)
                re, im, sq = response(j, r, b)
                total = total + wr * sq
                if j > 0:
                    zz[j - 1, 0, r, b - 1] = wr * re
                    zz[j - 1, 1, r, b - 1] = wr * im
                if j < 2:
                    mm[j, 4 + r, :, blk(b)] = jnp.sqrt(sq + EPS)
            if j < 2:
                for side, b in ((0, 0), (1, 9)):
                    sm[j, side, r] = jnp.sqrt(response(j, r, b)[2] + EPS)
            return total

        powers.append(lax.fori_loop(0, 8, row, jnp.zeros((8, 128), f32)))

    for j in range(2):
        for r in range(8):
            mm[j, 4 + r, :, blk(0)] = w_(f2, sm[j, 0, 7 - r], sm[j, 0, r])
            mm[j, 4 + r, :, blk(9)] = w_(f3, sm[j, 1, 7 - r], sm[j, 1, r])

        def rim_row(i, _, j=j):
            for r, dst, f in ((i, i, f0), (i + 4, i + 12, f1)):
                m = [jnp.sqrt(response(3 + j, r, b)[2] + EPS) for b in range(10)]
                mm[j, dst, :, blk(0)] = m[0]
                mm[j, dst, :, blk(9)] = m[9]
                for b in range(1, 9):
                    mm[j, dst, :, blk(b)] = w_(f, revl(m[9 - b]), m[b])
            return 0

        lax.fori_loop(0, 4, rim_row, 0)

    for q, (j1, j2) in enumerate(PAIRS):
        d = 2**j2
        first, last = lane < d, lane >= 128 - d

        def left(v):
            return pltpu.roll(w_(last, v[0], v[1]), d, 1)

        def right(v):
            return pltpu.roll(w_(first, v[2], v[1]), 128 - d, 1)

        def row2(r, carry, j1=j1, j2=j2, d=d, q=q, left=left, right=right):
            carry = list(carry)
            for b in range(1, 9):
                rows = [
                    tuple(mm[j1, r + (4 + s), :, blk(c)] for c in (b - 1, b, b + 1))
                    for s in (-d, 0, d)
                ]
                re, im = combos(features(*rows, left, right))
                wr = spread(wx, b - 1, r)
                energy = None
                for t in range(8):
                    zr = spread(zz, j2 - 1, 0, r, b - 1, t)
                    zi = spread(zz, j2 - 1, 1, r, b - 1, t)
                    carry[t] = carry[t] + (zr * re[t] + zi * im[t])
                    sq = re[t] * re[t] + im[t] * im[t]
                    carry[8 + t] = carry[8 + t] + wr * sq
                    energy = sq if energy is None else energy + sq
                if q == 1:
                    energy = energy + es[0, r, :, blk(b - 1)]
                es[q // 2, r, :, blk(b - 1)] = energy
            return tuple(carry)

        sums = lax.fori_loop(0, 8, row2, tuple(jnp.zeros((8, 128), f32) for _ in range(16)))
        for k in range(16):
            kind, t = divmod(k, 8)
            acc[pl.ds(q * 128 + kind * 64 + t, 8, stride=8), :] = sums[k]

    for r in range(8):
        en0[r : r + 1, :] = jnp.sum(es[0, r], axis=0, keepdims=True)
        en1[r : r + 1, :] = jnp.sum(es[1, r], axis=0, keepdims=True)

    lanes_summed = lax.dot_general(
        jnp.ones((8, 128), f32),
        acc[...],
        (((1,), (1,)), ((), ())),
        precision=lax.Precision.HIGHEST,
        preferred_element_type=f32,
    )
    w_sum = wx[0]
    for b in range(1, 8):
        w_sum = w_sum + wx[b]
    tail = jnp.zeros((1, 128), f32)
    for i, v in enumerate(powers + [w_sum]):
        tail = w_(lane[0:1] == i, jnp.sum(v), tail)
    for c in range(stats.shape[0]):
        for q in range(3):
            stats[c, q : q + 1, :] = lanes_summed[0:1, blk(q)]
        stats[c, 3:4, :] = tail


def middle_kernel(parts, out, *, n_y):
    x = lax.axis_index("x")
    total = parts[0]
    for i in range(1, parts.shape[0]):
        total = total + parts[i]
    mine = parts[x * n_y]
    for i in range(1, n_y):
        mine = mine + parts[x * n_y + i]
    for i in range(out.shape[0]):
        out[i, 0:4] = total
        out[i, 4:8] = mine


def final_kernel(parts, en0, en1, face_out, sky_out, energy, *, n_zl):
    first = (lax.axis_index("zh") * lax.axis_size("core") + lax.axis_index("core")) * n_zl
    total = parts[0, 0:4]
    for i in range(1, parts.shape[0]):
        total = total + parts[i, 0:4]
    mine = parts[first, 4:8]
    for i in range(1, n_zl):
        mine = mine + parts[first + i, 4:8]
    weight = total[3:4, 3:4]
    level = [total[3:4, j : j + 1] / (8.0 * weight) + EPS for j in range(3)]
    scale = [1.0 / jnp.sqrt(v) for v in level]
    lane = lax.broadcasted_iota(jnp.int32, (1, 128), 1)
    for q, (j1, j2) in enumerate(PAIRS):
        third = jnp.broadcast_to(scale[j1] * scale[j2], (1, 128))
        fourth = jnp.broadcast_to(1.0 / level[j1], (1, 128))
        factor = jnp.where(lane < 64, third, fourth)
        sky_out[q : q + 1, :] = total[q : q + 1] * (factor / weight)
        face_out[0, q : q + 1, :] = mine[q : q + 1] * (factor / mine[3:4, 3:4])
    a = jnp.broadcast_to(1.0 / (192.0 * level[0]), (8, 1024))
    b = jnp.broadcast_to(1.0 / (192.0 * level[1]), (8, 1024))
    energy[...] = en0[...] * a + en1[...] * b


def ring(value, axes, shift):
    n = lax.axis_size(axes)
    return lax.ppermute(value, axes, [(i, (i + shift) % n) for i in range(n)])


def on_device(dust, seam_flags, block_weights):
    f32 = jnp.float32
    sds = jax.ShapeDtypeStruct
    lane = lax.broadcasted_iota(jnp.int32, (8, 128), 1)
    flags = jnp.pad(seam_flags.reshape(1, 4).astype(f32), ((0, 0), (FLAG_LANE, 124 - FLAG_LANE)))
    pack = jnp.where(lane < 16, dust[:, :128], jnp.where(lane >= 112, dust[:, -128:], flags))
    left, right = ring(pack, PATCH, 1), ring(pack, PATCH, -1)
    message = jnp.concatenate([dust, pack, left, right], axis=1)
    above, below = ring(message, FACE, 1), ring(message, FACE, -1)
    n_y, n_zl = lax.axis_size("y"), lax.axis_size("zl")
    n_first, n_second = lax.axis_size(("x", "y")), lax.axis_size(("zh", "core", "zl"))
    stats, en0, en1 = pl.pallas_call(
        main_kernel,
        out_shape=(sds((n_first, 4, 128), f32), sds((8, 1024), f32), sds((8, 1024), f32)),
        scratch_shapes=[
            pltpu.VMEM((16, 1536), f32),
            pltpu.VMEM((16, 1536), f32),
            pltpu.VMEM((5, 8, 10, 8, 128), f32),
            pltpu.VMEM((2, 16, 8, 1280), f32),
            pltpu.VMEM((2, 2, 8, 8, 128), f32),
            pltpu.VMEM((2, 2, 8, 8, 8, 128), f32),
            pltpu.VMEM((8, 8, 128), f32),
            pltpu.VMEM((384, 128), f32),
            pltpu.VMEM((2, 8, 8, 1024), f32),
        ],
        name="both_layers",
    )(message, above, below, block_weights)
    stats = lax.all_to_all(stats, ("x", "y"), 0, 0, tiled=True)
    stats = pl.pallas_call(
        lambda *refs: middle_kernel(*refs, n_y=n_y),
        out_shape=sds((n_second, 8, 128), f32),
        name="row_part",
    )(stats)
    stats = lax.all_to_all(stats, ("zh", "core", "zl"), 0, 0, tiled=True)
    face_moments, sky_moments, energy = pl.pallas_call(
        lambda *refs: final_kernel(*refs, n_zl=n_zl),
        out_shape=(sds((1, 3, 128), f32), sds((3, 128), f32), sds((8, 1024), f32)),
        name="finish",
    )(stats, en0, en1)
    return energy, face_moments, sky_moments


def solution(mesh):
    fine = Mesh(mesh.devices.reshape(4, 2, 2, 4, 8), FACE + PATCH)
    return jax.shard_map(
        on_device,
        mesh=fine,
        in_specs=(P(FACE, PATCH), P(FACE, PATCH, None), P(FACE, PATCH)),
        out_specs=(P(FACE, PATCH), P(FACE, None, None), P()),
        check_vma=False,
    )
```

```python
import math

import jax
import jax.numpy as jnp
import numpy as np
from jax import lax
from jax.experimental import pallas as pl
from jax.experimental.pallas import tpu as pltpu
from jax.sharding import Mesh
from jax.sharding import PartitionSpec as P

EPS = 1e-06
PAIRS = ((0, 1), (0, 2), (1, 2))
FACE = ("x", "zh", "core")
PATCH = ("zl", "y")
FLAG_LANE = 32


def filter_features():
    rows = np.repeat(np.array([-1.0, 0.0, 1.0]), 3)
    cols = np.tile(np.array([-1.0, 0.0, 1.0]), 3)
    env = np.exp(-(rows**2 + cols**2) / 1.28)
    at = {(int(a), int(b)): i for i, (a, b) in enumerate(zip(rows, cols))}
    picks = [at[0, 1], at[1, 0], at[1, 1], at[1, -1]]
    even, odd = [], []
    for t in range(8):
        h = math.pi * t / 8.0
        ph = 2.2 * (rows * math.cos(h) + cols * math.sin(h))
        c = np.cos(ph) - np.sum(env * np.cos(ph)) / np.sum(env)
        s = np.sin(ph) - np.sum(env * np.sin(ph)) / np.sum(env)
        norm = np.sqrt(np.sum(env**2 * (c**2 + s**2)))
        for src, dst in ((env * c / norm, even), (env * s / norm, odd)):
            v = src[picks]
            dst.append([v[0], v[1], (v[2] + v[3]) / 2, (v[2] - v[3]) / 2])
    out = np.array([even, odd])
    out[np.abs(out) < 1e-12] = 0.0
    return out


TABLE = filter_features()


def features(top, mid, bot, left, right):
    tl, tr = left(top), right(top)
    ml, mr = left(mid), right(mid)
    bl, br = left(bot), right(bot)
    top, mid, bot = (v[len(v) // 2] if isinstance(v, tuple) else v for v in (top, mid, bot))
    two = mid + mid
    s1, s2 = br + tl, bl + tr
    d1, d2 = br - tl, bl - tr
    return (
        ml + mr - two,
        top + bot - two,
        s1 + s2 - (two + two),
        s1 - s2,
        mr - ml,
        bot - top,
        d1 + d2,
        d1 - d2,
    )


def combos(ft):
    e01, e10, p, q, o01, o10, po, qo = ft

    def lin(pairs):
        total = None
        for c, v in pairs:
            if c == 0.0:
                continue
            term = float(c) * v
            total = term if total is None else total + term
        return total

    re, im = [None] * 8, [None] * 8
    for t in (0, 4):
        ce, co = TABLE[0, t], TABLE[1, t]
        re[t] = lin(zip(ce, (e01, e10, p, q)))
        im[t] = lin(zip(co, (o01, o10, po, qo)))
    for t in (1, 2, 3):
        ce, co = TABLE[0, t], TABLE[1, t]
        a, b = lin(zip(ce[:3], (e01, e10, p))), lin([(ce[3], q)])
        re[t], re[8 - t] = a + b, a - b
        a = lin([(co[0], o01), (co[3], qo)])
        b = lin([(co[1], o10), (co[2], po)])
        im[t], im[8 - t] = a + b, a - b
    return re, im


def edge_pack(tile):
    lane = lax.broadcasted_iota(jnp.int32, (8, 128), 1)
    edges = jnp.where(lane < 64, tile[:, 0:128], tile[:, 896:1024])
    return jnp.where((lane < 16) | (lane >= 112), edges, tile[:, 1024:1152])


def tile_kernel(dust, flags, out, bits, sems):
    tile_copy = pltpu.make_async_copy(dust, out.at[:, pl.ds(0, 1024)], sems.at[0])
    flag_copy = pltpu.make_async_copy(flags, bits, sems.at[1])
    tile_copy.start()
    flag_copy.start()
    lane = lax.broadcasted_iota(jnp.int32, (8, 128), 1)
    row = jnp.zeros((8, 128), jnp.float32)
    flag_copy.wait()
    for i in range(4):
        row = jnp.where(lane == FLAG_LANE + i, bits[0, 0, i].astype(jnp.float32), row)
    out[:, 1024:1152] = row
    tile_copy.wait()


def sorted_pair(near, far, odd):
    return jnp.where(odd, near, far), jnp.where(odd, far, near)


def pack_kernel(own, near, far, out):
    out[:, 0:128] = edge_pack(own)
    a, b = sorted_pair(edge_pack(near), edge_pack(far), lax.axis_index("core") == 1)
    out[:, 128:256] = a
    out[:, 256:384] = b


def main_kernel(own, near_f, far_f, packs, near_p, far_p, bw, stats, en0, en1, xt, xud, fe, mm, sm, zz, wx, acc, es):
    f32 = jnp.float32
    lane = lax.broadcasted_iota(jnp.int32, (8, 128), 1)
    sub = lax.broadcasted_iota(jnp.int32, (8, 128), 0)
    low = lane < 64
    back_lane, back_row = 127 - lane, 7 - sub

    def revl(v):
        return jnp.take_along_axis(v, back_lane, axis=1, mode="promise_in_bounds")

    def revr(v):
        return jnp.take_along_axis(v, back_row, axis=0, mode="promise_in_bounds")

    def flag(pack, i):
        return jnp.broadcast_to(pack[:, FLAG_LANE + i : FLAG_LANE + i + 1], (8, 128)) > 0.5

    odd_f = lax.axis_index("core") == 1
    odd_p = lax.axis_index("y") % 2 == 1
    pt, pu, pd = (packs[:, 128 * i : 128 * i + 128] for i in range(3))
    sides = [
        sorted_pair(near_p[:, 128 * i : 128 * i + 128], far_p[:, 128 * i : 128 * i + 128], odd_p)
        for i in range(3)
    ]
    (plf, prt), (pul, pur), (pdl, pdr) = sides
    w_ = jnp.where
    turn_t, turn_u, turn_d = revr(pt), revr(pu), revr(pd)
    revl_l, revl_r = revl(plf), revl(prt)
    f0, f1, f2, f3 = (flag(pt, i) for i in range(4))

    grow = lax.broadcasted_iota(jnp.int32, (128, 1024), 1) // 8 == lax.broadcasted_iota(
        jnp.int32, (128, 1024), 0
    )
    wide = jnp.dot(
        bw[...].astype(jnp.bfloat16), grow.astype(jnp.bfloat16), preferred_element_type=f32
    )
    for b in range(8):
        wx[b] = wide[:, 128 * b : 128 * b + 128]

    def blk(b):
        return slice(128 * b, 128 * b + 128)

    f0d, f1u = flag(pd, 0), flag(pu, 1)
    for b in range(8):
        t_b, t_r = own[:, blk(b)], revl(own[:, blk(7 - b)])
        u_b, d_b = sorted_pair(near_f[:, blk(b)], far_f[:, blk(b)], odd_f)
        u_r, d_r = sorted_pair(near_f[:, blk(7 - b)], far_f[:, blk(7 - b)], odd_f)
        u_r, d_r = revl(u_r), revl(d_r)
        xt[4:12, blk(b + 1)] = t_b
        xt[0:4, blk(b + 1)] = w_(f0, u_r, u_b)[4:8]
        xt[12:16, blk(b + 1)] = w_(f1, d_r, d_b)[0:4]
        xud[0:6, blk(b + 1)] = u_b[2:8]
        xud[6:8, blk(b + 1)] = w_(f1u, t_r, t_b)[0:2]
        xud[8:10, blk(b + 1)] = w_(f0d, t_r, t_b)[6:8]
        xud[10:16, blk(b + 1)] = d_b[0:6]
    xt[4:12, blk(0)] = w_(f2, revr(plf), plf)
    xt[0:4, blk(0)] = pul[4:8]
    xt[12:16, blk(0)] = pdl[0:4]
    xt[4:12, blk(9)] = w_(f3, revr(prt), prt)
    xt[0:4, blk(9)] = pur[4:8]
    xt[12:16, blk(9)] = pdr[0:4]
    xud[0:6, blk(0)] = w_(flag(pu, 2), revr(pul), pul)[2:8]
    xud[6:8, blk(0)] = plf[0:2]
    xud[8:10, blk(0)] = plf[6:8]
    xud[10:16, blk(0)] = w_(flag(pd, 2), revr(pdl), pdl)[0:6]
    xud[0:6, blk(9)] = w_(flag(pu, 3), revr(pur), pur)[2:8]
    xud[6:8, blk(9)] = prt[0:2]
    xud[8:10, blk(9)] = prt[6:8]
    xud[10:16, blk(9)] = w_(flag(pd, 3), revr(pdr), pdr)[0:6]
    xt[4:12, blk(10)] = w_(low, w_(flag(plf, 3), turn_t, pt), plf)
    xt[0:4, blk(10)] = w_(low, pu, w_(flag(plf, 0), revl(pul), pul))[4:8]
    xt[12:16, blk(10)] = w_(low, pd, w_(flag(plf, 1), revl(pdl), pdl))[0:4]
    xt[4:12, blk(11)] = w_(low, prt, w_(flag(prt, 2), turn_t, pt))
    xt[0:4, blk(11)] = w_(low, w_(flag(prt, 0), revl(pur), pur), pu)[4:8]
    xt[12:16, blk(11)] = w_(low, w_(flag(prt, 1), revl(pdr), pdr), pd)[0:4]
    xud[0:6, blk(10)] = w_(low, w_(flag(pul, 3), turn_u, pu), pul)[2:8]
    xud[6:8, blk(10)] = w_(low, pt, w_(flag(pul, 1), revl_l, plf))[0:2]
    xud[8:10, blk(10)] = w_(low, pt, w_(flag(pdl, 0), revl_l, plf))[6:8]
    xud[10:16, blk(10)] = w_(low, w_(flag(pdl, 3), turn_d, pd), pdl)[0:6]
    xud[0:6, blk(11)] = w_(low, pur, w_(flag(pur, 2), turn_u, pu))[2:8]
    xud[6:8, blk(11)] = w_(low, w_(flag(pur, 1), revl_r, prt), pt)[0:2]
    xud[8:10, blk(11)] = w_(low, w_(flag(pdr, 0), revl_r, prt), pt)[6:8]
    xud[10:16, blk(11)] = w_(low, pdr, w_(flag(pdr, 2), turn_d, pd))[0:6]

    def store_features(slot, load, d):
        first, last = lane < d, lane >= 128 - d

        def left(v):
            return pltpu.roll(w_(last, v[0], v[1]), d, 1)

        def right(v):
            return pltpu.roll(w_(first, v[2], v[1]), 128 - d, 1)

        def left1(v):
            return pltpu.roll(v, d, 1)

        def right1(v):
            return pltpu.roll(v, 128 - d, 1)

        for b in range(1, 9):
            rows = [tuple(load(s, c) for c in (b - 1, b, b + 1)) for s in (-d, 0, d)]
            for k, v in enumerate(features(*rows, left, right)):
                fe[slot, k, b] = v
        if d < 4:
            for b, dst in ((10, 0), (11, 9)):
                rows = [load(s, b) for s in (-d, 0, d)]
                for k, v in enumerate(features(*rows, left1, right1)):
                    fe[slot, k, dst] = v

    def load_own(s, b):
        return xt[4 + s : 12 + s, blk(b)]

    def load_ud(s, b):
        return jnp.concatenate([xud[2 + s : 6 + s, blk(b)], xud[10 + s : 14 + s, blk(b)]], 0)

    for j in range(3):
        store_features(j, load_own, 2**j)
    for j in range(2):
        store_features(3 + j, load_ud, 2**j)

    def column(vals):
        out = jnp.full((8, 128), float(vals[0]), f32)
        for t in range(1, 8):
            out = w_(sub == t, float(vals[t]), out)
        return out

    ce = [column(TABLE[0, :, k]) for k in range(4)]
    co = [column(TABLE[1, :, k]) for k in range(4)]

    def spread(ref, *at):
        *lead, r = at
        return ref[(*lead, pl.ds(r, 8, stride=0), slice(None))]

    def response(slot, r, b):
        v = [spread(fe, slot, k, b, r) for k in range(8)]
        re = ce[0] * v[0] + ce[1] * v[1] + (ce[2] * v[2] + ce[3] * v[3])
        im = co[0] * v[4] + co[1] * v[5] + (co[2] * v[6] + co[3] * v[7])
        return re, im, re * re + im * im

    powers = []
    for j in range(3):

        def row(r, total, j=j):
            for b in range(1, 9):
                wr = spread(wx, b - 1, r)
                re, im, sq = response(j, r, b)
                total = total + wr * sq
                if j > 0:
                    zz[j - 1, 0, r, b - 1] = wr * re
                    zz[j - 1, 1, r, b - 1] = wr * im
                if j < 2:
                    mm[j, 4 + r, :, blk(b)] = jnp.sqrt(sq + EPS)
            if j < 2:
                for side, b in ((0, 0), (1, 9)):
                    sm[j, side, r] = jnp.sqrt(response(j, r, b)[2] + EPS)
            return total

        powers.append(lax.fori_loop(0, 8, row, jnp.zeros((8, 128), f32)))

    for j in range(2):
        for r in range(8):
            mm[j, 4 + r, :, blk(0)] = w_(f2, sm[j, 0, 7 - r], sm[j, 0, r])
            mm[j, 4 + r, :, blk(9)] = w_(f3, sm[j, 1, 7 - r], sm[j, 1, r])

        def rim_row(i, _, j=j):
            for r, dst, f in ((i, i, f0), (i + 4, i + 12, f1)):
                m = [jnp.sqrt(response(3 + j, r, b)[2] + EPS) for b in range(10)]
                mm[j, dst, :, blk(0)] = m[0]
                mm[j, dst, :, blk(9)] = m[9]
                for b in range(1, 9):
                    mm[j, dst, :, blk(b)] = w_(f, revl(m[9 - b]), m[b])
            return 0

        lax.fori_loop(0, 4, rim_row, 0)

    for q, (j1, j2) in enumerate(PAIRS):
        d = 2**j2
        first, last = lane < d, lane >= 128 - d

        def left(v):
            return pltpu.roll(w_(last, v[0], v[1]), d, 1)

        def right(v):
            return pltpu.roll(w_(first, v[2], v[1]), 128 - d, 1)

        def row2(r, carry, j1=j1, j2=j2, d=d, q=q, left=left, right=right):
            carry = list(carry)
            for b in range(1, 9):
                rows = [
                    tuple(mm[j1, r + (4 + s), :, blk(c)] for c in (b - 1, b, b + 1))
                    for s in (-d, 0, d)
                ]
                re, im = combos(features(*rows, left, right))
                wr = spread(wx, b - 1, r)
                energy = None
                for t in range(8):
                    zr = spread(zz, j2 - 1, 0, r, b - 1, t)
                    zi = spread(zz, j2 - 1, 1, r, b - 1, t)
                    carry[t] = carry[t] + (zr * re[t] + zi * im[t])
                    sq = re[t] * re[t] + im[t] * im[t]
                    carry[8 + t] = carry[8 + t] + wr * sq
                    energy = sq if energy is None else energy + sq
                if q == 1:
                    energy = energy + es[0, r, :, blk(b - 1)]
                es[q // 2, r, :, blk(b - 1)] = energy
            return tuple(carry)

        sums = lax.fori_loop(0, 8, row2, tuple(jnp.zeros((8, 128), f32) for _ in range(16)))
        for k in range(16):
            kind, t = divmod(k, 8)
            acc[pl.ds(q * 128 + kind * 64 + t, 8, stride=8), :] = sums[k]

    for r in range(8):
        en0[r : r + 1, :] = jnp.sum(es[0, r], axis=0, keepdims=True)
        en1[r : r + 1, :] = jnp.sum(es[1, r], axis=0, keepdims=True)

    lanes_summed = lax.dot_general(
        jnp.ones((8, 128), f32),
        acc[...],
        (((1,), (1,)), ((), ())),
        precision=lax.Precision.HIGHEST,
        preferred_element_type=f32,
    )
    w_sum = wx[0]
    for b in range(1, 8):
        w_sum = w_sum + wx[b]
    tail = jnp.zeros((1, 128), f32)
    for i, v in enumerate(powers + [w_sum]):
        tail = w_(lane[0:1] == i, jnp.sum(v), tail)
    for c in range(stats.shape[0]):
        for q in range(3):
            stats[c, q : q + 1, :] = lanes_summed[0:1, blk(q)]
        stats[c, 3:4, :] = tail


def middle_kernel(parts, out, *, n_y):
    x = lax.axis_index("x")
    total = parts[0]
    for i in range(1, parts.shape[0]):
        total = total + parts[i]
    mine = parts[x * n_y]
    for i in range(1, n_y):
        mine = mine + parts[x * n_y + i]
    for i in range(out.shape[0]):
        out[i, 0:4] = total
        out[i, 4:8] = mine


def final_kernel(parts, en0, en1, face_out, sky_out, energy, *, n_zl):
    first = (lax.axis_index("zh") * lax.axis_size("core") + lax.axis_index("core")) * n_zl
    total = parts[0, 0:4]
    for i in range(1, parts.shape[0]):
        total = total + parts[i, 0:4]
    mine = parts[first, 4:8]
    for i in range(1, n_zl):
        mine = mine + parts[first + i, 4:8]
    weight = total[3:4, 3:4]
    level = [total[3:4, j : j + 1] / (8.0 * weight) + EPS for j in range(3)]
    scale = [1.0 / jnp.sqrt(v) for v in level]
    lane = lax.broadcasted_iota(jnp.int32, (1, 128), 1)
    for q, (j1, j2) in enumerate(PAIRS):
        third = jnp.broadcast_to(scale[j1] * scale[j2], (1, 128))
        fourth = jnp.broadcast_to(1.0 / level[j1], (1, 128))
        factor = jnp.where(lane < 64, third, fourth)
        sky_out[q : q + 1, :] = total[q : q + 1] * (factor / weight)
        face_out[q, 0:1, :] = mine[q : q + 1] * (factor / mine[3:4, 3:4])
    a = jnp.broadcast_to(1.0 / (192.0 * level[0]), (8, 1024))
    b = jnp.broadcast_to(1.0 / (192.0 * level[1]), (8, 1024))
    energy[...] = en0[...] * a + en1[...] * b


def pair_exchange(value, axes):
    n = lax.axis_size(axes)
    far = lax.ppermute(value, axes, [(i, (i + (1 if i % 2 else n - 1)) % n) for i in range(n)])
    near = lax.ppermute(value, axes, [(i, i ^ 1) for i in range(n)])
    return near, far


def on_device(dust, seam_flags, block_weights):
    f32 = jnp.float32
    sds = jax.ShapeDtypeStruct
    vmem = pl.BlockSpec(memory_space=pltpu.VMEM)
    hbm = pl.BlockSpec(memory_space=pltpu.HBM)
    tile = pl.pallas_call(
        tile_kernel,
        out_shape=sds((8, 1152), f32),
        in_specs=[hbm, hbm],
        out_specs=vmem,
        scratch_shapes=[pltpu.SMEM((1, 1, 4), jnp.int32), pltpu.SemaphoreType.DMA((2,))],
        compiler_params=pltpu.CompilerParams(vmem_limit_bytes=2 << 20),
        name="tile_and_flags",
    )(*(pltpu.with_memory_space_constraint(v, pltpu.HBM) for v in (dust, seam_flags)))
    near_f, far_f = pair_exchange(tile, FACE)
    packs = pl.pallas_call(
        pack_kernel,
        out_shape=sds((8, 384), f32),
        in_specs=[vmem] * 3,
        out_specs=vmem,
        compiler_params=pltpu.CompilerParams(vmem_limit_bytes=2 << 20),
        name="edge_packs",
    )(tile, near_f, far_f)
    near_p, far_p = pair_exchange(packs, PATCH)
    n_y, n_zl = lax.axis_size("y"), lax.axis_size("zl")
    n_first, n_second = lax.axis_size(("x", "y")), lax.axis_size(("zh", "core", "zl"))
    stats, en0, en1 = pl.pallas_call(
        main_kernel,
        out_shape=(sds((n_first, 4, 128), f32), sds((8, 1024), f32), sds((8, 1024), f32)),
        in_specs=[vmem] * 7,
        out_specs=(vmem,) * 3,
        scratch_shapes=[
            pltpu.VMEM((16, 1536), f32),
            pltpu.VMEM((16, 1536), f32),
            pltpu.VMEM((5, 8, 10, 8, 128), f32),
            pltpu.VMEM((2, 16, 8, 1280), f32),
            pltpu.VMEM((2, 2, 8, 8, 128), f32),
            pltpu.VMEM((2, 2, 8, 8, 8, 128), f32),
            pltpu.VMEM((8, 8, 128), f32),
            pltpu.VMEM((384, 128), f32),
            pltpu.VMEM((2, 8, 8, 1024), f32),
        ],
        compiler_params=pltpu.CompilerParams(vmem_limit_bytes=14 << 20),
        name="both_layers",
    )(tile, near_f, far_f, packs, near_p, far_p, block_weights)
    stats = lax.all_to_all(stats, ("x", "y"), 0, 0, tiled=True)
    stats = pl.pallas_call(
        lambda *refs: middle_kernel(*refs, n_y=n_y),
        out_shape=sds((n_second, 8, 128), f32),
        in_specs=[vmem],
        out_specs=vmem,
        compiler_params=pltpu.CompilerParams(vmem_limit_bytes=2 << 20),
        name="row_part",
    )(stats)
    stats = lax.all_to_all(stats, ("zh", "core", "zl"), 0, 0, tiled=True)
    face_moments, sky_moments, energy = pl.pallas_call(
        lambda *refs: final_kernel(*refs, n_zl=n_zl),
        out_shape=(sds((3, 1, 128), f32), sds((3, 128), f32), sds((8, 1024), f32)),
        in_specs=[vmem] * 3,
        out_specs=(vmem,) * 3,
        compiler_params=pltpu.CompilerParams(vmem_limit_bytes=2 << 20),
        name="finish",
    )(stats, en0, en1)
    return energy, jnp.swapaxes(face_moments, 0, 1), sky_moments


def solution(mesh):
    fine = Mesh(mesh.devices.reshape(4, 2, 2, 4, 8), FACE + PATCH)
    return jax.shard_map(
        on_device,
        mesh=fine,
        in_specs=(P(FACE, PATCH), P(FACE, PATCH, None), P(FACE, PATCH)),
        out_specs=(P(FACE, PATCH), P(FACE, None, None), P()),
        check_vma=False,
    )
```

```python
import math

import jax
import jax.numpy as jnp
import numpy as np
from jax import lax
from jax.experimental import pallas as pl
from jax.experimental.pallas import tpu as pltpu
from jax.sharding import Mesh
from jax.sharding import PartitionSpec as P

EPS = 1e-06
PAIRS = ((0, 1), (0, 2), (1, 2))
FACE = ("x", "zh", "core")
PATCH = ("zl", "y")
FLAG_LANE = 32


def filter_features():
    rows = np.repeat(np.array([-1.0, 0.0, 1.0]), 3)
    cols = np.tile(np.array([-1.0, 0.0, 1.0]), 3)
    env = np.exp(-(rows**2 + cols**2) / 1.28)
    at = {(int(a), int(b)): i for i, (a, b) in enumerate(zip(rows, cols))}
    picks = [at[0, 1], at[1, 0], at[1, 1], at[1, -1]]
    even, odd = [], []
    for t in range(8):
        h = math.pi * t / 8.0
        ph = 2.2 * (rows * math.cos(h) + cols * math.sin(h))
        c = np.cos(ph) - np.sum(env * np.cos(ph)) / np.sum(env)
        s = np.sin(ph) - np.sum(env * np.sin(ph)) / np.sum(env)
        norm = np.sqrt(np.sum(env**2 * (c**2 + s**2)))
        for src, dst in ((env * c / norm, even), (env * s / norm, odd)):
            v = src[picks]
            dst.append([v[0], v[1], (v[2] + v[3]) / 2, (v[2] - v[3]) / 2])
    out = np.array([even, odd])
    out[np.abs(out) < 1e-12] = 0.0
    return out


TABLE = filter_features()


def features(top, mid, bot, left, right):
    tl, tr = left(top), right(top)
    ml, mr = left(mid), right(mid)
    bl, br = left(bot), right(bot)
    top, mid, bot = (v[len(v) // 2] if isinstance(v, tuple) else v for v in (top, mid, bot))
    two = mid + mid
    s1, s2 = br + tl, bl + tr
    d1, d2 = br - tl, bl - tr
    return (
        ml + mr - two,
        top + bot - two,
        s1 + s2 - (two + two),
        s1 - s2,
        mr - ml,
        bot - top,
        d1 + d2,
        d1 - d2,
    )


def combos(ft):
    e01, e10, p, q, o01, o10, po, qo = ft

    def lin(pairs):
        total = None
        for c, v in pairs:
            if c == 0.0:
                continue
            term = float(c) * v
            total = term if total is None else total + term
        return total

    re, im = [None] * 8, [None] * 8
    for t in (0, 4):
        ce, co = TABLE[0, t], TABLE[1, t]
        re[t] = lin(zip(ce, (e01, e10, p, q)))
        im[t] = lin(zip(co, (o01, o10, po, qo)))
    for t in (1, 2, 3):
        ce, co = TABLE[0, t], TABLE[1, t]
        a, b = lin(zip(ce[:3], (e01, e10, p))), lin([(ce[3], q)])
        re[t], re[8 - t] = a + b, a - b
        a = lin([(co[0], o01), (co[3], qo)])
        b = lin([(co[1], o10), (co[2], po)])
        im[t], im[8 - t] = a + b, a - b
    return re, im


def edge_pack(tile):
    lane = lax.broadcasted_iota(jnp.int32, (8, 128), 1)
    edges = jnp.where(lane < 64, tile[:, 0:128], tile[:, 896:1024])
    return jnp.where((lane < 16) | (lane >= 112), edges, tile[:, 1024:1152])


def tile_kernel(dust, flags, out, bits, sems):
    tile_copy = pltpu.make_async_copy(dust, out.at[:, pl.ds(0, 1024)], sems.at[0])
    flag_copy = pltpu.make_async_copy(flags, bits, sems.at[1])
    tile_copy.start()
    flag_copy.start()
    lane = lax.broadcasted_iota(jnp.int32, (8, 128), 1)
    row = jnp.zeros((8, 128), jnp.float32)
    flag_copy.wait()
    for i in range(4):
        row = jnp.where(lane == FLAG_LANE + i, bits[0, 0, i].astype(jnp.float32), row)
    out[:, 1024:1152] = row
    tile_copy.wait()


def sorted_pair(near, far, odd):
    return jnp.where(odd, near, far), jnp.where(odd, far, near)


def pack_kernel(own, near, far, out):
    out[:, 0:128] = edge_pack(own)
    a, b = sorted_pair(edge_pack(near), edge_pack(far), lax.axis_index("core") == 1)
    out[:, 128:256] = a
    out[:, 256:384] = b


def blk(b):
    return slice(128 * b, 128 * b + 128)


def lanes():
    return lax.broadcasted_iota(jnp.int32, (8, 128), 1)


def rows_of():
    return lax.broadcasted_iota(jnp.int32, (8, 128), 0)


def revl(v):
    return jnp.take_along_axis(v, 127 - lanes(), axis=1, mode="promise_in_bounds")


def revr(v):
    return jnp.take_along_axis(v, 7 - rows_of(), axis=0, mode="promise_in_bounds")


def flag(pack, i):
    return jnp.broadcast_to(pack[:, FLAG_LANE + i : FLAG_LANE + i + 1], (8, 128)) > 0.5


def spread(ref, *at):
    *lead, r = at
    return ref[(*lead, pl.ds(r, 8, stride=0), slice(None))]


def place_tiles(own, near_f, far_f, packs, xt, xud, blocks):
    odd_f = lax.axis_index("core") == 1
    pt, pu, pd = (packs[:, blk(i)] for i in range(3))
    f0, f1, f0d, f1u = flag(pt, 0), flag(pt, 1), flag(pd, 0), flag(pu, 1)
    for b in blocks:
        b, c = b - 1, 8 - b
        t_b, t_r = own[:, blk(b)], revl(own[:, blk(c)])
        u_b, d_b = sorted_pair(near_f[:, blk(b)], far_f[:, blk(b)], odd_f)
        u_r, d_r = sorted_pair(near_f[:, blk(c)], far_f[:, blk(c)], odd_f)
        u_r, d_r = revl(u_r), revl(d_r)
        xt[4:12, blk(b + 1)] = t_b
        xt[0:4, blk(b + 1)] = jnp.where(f0, u_r, u_b)[4:8]
        xt[12:16, blk(b + 1)] = jnp.where(f1, d_r, d_b)[0:4]
        xud[0:6, blk(b + 1)] = u_b[2:8]
        xud[6:8, blk(b + 1)] = jnp.where(f1u, t_r, t_b)[0:2]
        xud[8:10, blk(b + 1)] = jnp.where(f0d, t_r, t_b)[6:8]
        xud[10:16, blk(b + 1)] = d_b[0:6]


def place_rims(packs, near_p, far_p, xt, xud):
    low = lanes() < 64
    odd_p = lax.axis_index("y") % 2 == 1
    pt, pu, pd = (packs[:, blk(i)] for i in range(3))
    (plf, prt), (pul, pur), (pdl, pdr) = (
        sorted_pair(near_p[:, blk(i)], far_p[:, blk(i)], odd_p) for i in range(3)
    )
    w_ = jnp.where
    turn_t, turn_u, turn_d = revr(pt), revr(pu), revr(pd)
    revl_l, revl_r = revl(plf), revl(prt)
    xt[4:12, blk(0)] = w_(flag(pt, 2), revr(plf), plf)
    xt[0:4, blk(0)] = pul[4:8]
    xt[12:16, blk(0)] = pdl[0:4]
    xt[4:12, blk(9)] = w_(flag(pt, 3), revr(prt), prt)
    xt[0:4, blk(9)] = pur[4:8]
    xt[12:16, blk(9)] = pdr[0:4]
    xud[0:6, blk(0)] = w_(flag(pu, 2), revr(pul), pul)[2:8]
    xud[6:8, blk(0)] = plf[0:2]
    xud[8:10, blk(0)] = plf[6:8]
    xud[10:16, blk(0)] = w_(flag(pd, 2), revr(pdl), pdl)[0:6]
    xud[0:6, blk(9)] = w_(flag(pu, 3), revr(pur), pur)[2:8]
    xud[6:8, blk(9)] = prt[0:2]
    xud[8:10, blk(9)] = prt[6:8]
    xud[10:16, blk(9)] = w_(flag(pd, 3), revr(pdr), pdr)[0:6]
    xt[4:12, blk(10)] = w_(low, w_(flag(plf, 3), turn_t, pt), plf)
    xt[0:4, blk(10)] = w_(low, pu, w_(flag(plf, 0), revl(pul), pul))[4:8]
    xt[12:16, blk(10)] = w_(low, pd, w_(flag(plf, 1), revl(pdl), pdl))[0:4]
    xt[4:12, blk(11)] = w_(low, prt, w_(flag(prt, 2), turn_t, pt))
    xt[0:4, blk(11)] = w_(low, w_(flag(prt, 0), revl(pur), pur), pu)[4:8]
    xt[12:16, blk(11)] = w_(low, w_(flag(prt, 1), revl(pdr), pdr), pd)[0:4]
    xud[0:6, blk(10)] = w_(low, w_(flag(pul, 3), turn_u, pu), pul)[2:8]
    xud[6:8, blk(10)] = w_(low, pt, w_(flag(pul, 1), revl_l, plf))[0:2]
    xud[8:10, blk(10)] = w_(low, pt, w_(flag(pdl, 0), revl_l, plf))[6:8]
    xud[10:16, blk(10)] = w_(low, w_(flag(pdl, 3), turn_d, pd), pdl)[0:6]
    xud[0:6, blk(11)] = w_(low, pur, w_(flag(pur, 2), turn_u, pu))[2:8]
    xud[6:8, blk(11)] = w_(low, w_(flag(pur, 1), revl_r, prt), pt)[0:2]
    xud[8:10, blk(11)] = w_(low, w_(flag(pdr, 0), revl_r, prt), pt)[6:8]
    xud[10:16, blk(11)] = w_(low, pdr, w_(flag(pdr, 2), turn_d, pd))[0:6]


def dust_features(xt, xud, fe, mains, sides):
    def load_own(s, b):
        return xt[4 + s : 12 + s, blk(b)]

    def load_ud(s, b):
        return jnp.concatenate([xud[2 + s : 6 + s, blk(b)], xud[10 + s : 14 + s, blk(b)]], 0)

    for slot, load, d in ((0, load_own, 1), (1, load_own, 2), (2, load_own, 4), (3, load_ud, 1), (4, load_ud, 2)):
        left, right = shifts(d)
        for b in mains:
            rows = [tuple(load(s, c) for c in (b - 1, b, b + 1)) for s in (-d, 0, d)]
            for k, v in enumerate(features(*rows, left, right)):
                fe[slot, k, b] = v
        if d == 4:
            continue
        for b, dst in sides:
            rows = [load(s, b) for s in (-d, 0, d)]
            turn_l, turn_r = (lambda v: pltpu.roll(v, d, 1)), (lambda v: pltpu.roll(v, 128 - d, 1))
            for k, v in enumerate(features(*rows, turn_l, turn_r)):
                fe[slot, k, dst] = v


def shifts(d):
    lane = lanes()
    first, last = lane < d, lane >= 128 - d

    def left(v):
        return pltpu.roll(jnp.where(last, v[0], v[1]), d, 1)

    def right(v):
        return pltpu.roll(jnp.where(first, v[2], v[1]), 128 - d, 1)

    return left, right


def first_layer(fe, wx, blocks, sides, put_m, put_side, put_z, flips, start):
    sub = rows_of()

    def column(vals):
        out = jnp.full((8, 128), float(vals[0]), jnp.float32)
        for t in range(1, 8):
            out = jnp.where(sub == t, float(vals[t]), out)
        return out

    ce = [column(TABLE[0, :, k]) for k in range(4)]
    co = [column(TABLE[1, :, k]) for k in range(4)]

    def response(slot, r, b):
        v = [spread(fe, slot, k, b, r) for k in range(8)]
        re = ce[0] * v[0] + ce[1] * v[1] + (ce[2] * v[2] + ce[3] * v[3])
        im = co[0] * v[4] + co[1] * v[5] + (co[2] * v[6] + co[3] * v[7])
        return re, im, re * re + im * im

    powers = []
    for j in range(3):

        def row(r, total, j=j):
            for b in blocks:
                wr = spread(wx, b - 1, r)
                re, im, sq = response(j, r, b)
                total = total + wr * sq
                if j > 0:
                    put_z(j, r, b, wr * re, wr * im)
                if j < 2:
                    put_m(j, 4 + r, b, jnp.sqrt(sq + EPS))
            if j < 2:
                for b in sides:
                    put_side(j, r, b, jnp.sqrt(response(j, r, b)[2] + EPS))
            return total

        powers.append(lax.fori_loop(0, 8, row, start[j]))
    for j in range(2):

        def rim_row(i, _, j=j):
            for r, dst, f in ((i, i, flips[0]), (i + 4, i + 12, flips[1])):
                m = {b: jnp.sqrt(response(3 + j, r, b)[2] + EPS) for b in (*blocks, *sides)}
                for b in blocks:
                    put_m(j, dst, b, jnp.where(f, revl(m[9 - b]), m[b]))
                for b in sides:
                    put_m(j, dst, b, m[b])
            return 0

        lax.fori_loop(0, 4, rim_row, 0)
    return powers


def second_layer(q, blocks, get_m, get_z, wx, put_energy, start):
    j1, j2 = PAIRS[q]
    d = 2**j2
    left, right = shifts(d)

    def row(r, carry):
        carry = list(carry)
        for b in blocks:
            rows = [tuple(get_m(j1, r + (4 + s), c) for c in (b - 1, b, b + 1)) for s in (-d, 0, d)]
            re, im = combos(features(*rows, left, right))
            wr = spread(wx, b - 1, r)
            energy = None
            for t in range(8):
                carry[t] = carry[t] + (get_z(j2, 0, r, b, t) * re[t] + get_z(j2, 1, r, b, t) * im[t])
                sq = re[t] * re[t] + im[t] * im[t]
                carry[8 + t] = carry[8 + t] + wr * sq
                energy = sq if energy is None else energy + sq
            put_energy(q, r, b, energy)
        return tuple(carry)

    return lax.fori_loop(0, 8, row, tuple(start))


INNER = (2, 3, 4, 5, 6, 7)
OUTER = (1, 8)
CORE = (3, 4, 5, 6)
EDGE = {0: 0, 1: 1, 8: 2, 9: 3}


def inner_kernel(own, near_f, far_f, packs, bw, mm, zz, wx, powers, sums, energies, xt, xud, fe):
    f32 = jnp.float32
    grow = lax.broadcasted_iota(jnp.int32, (128, 1024), 1) // 8 == lax.broadcasted_iota(
        jnp.int32, (128, 1024), 0
    )
    wide = jnp.dot(
        bw[...].astype(jnp.bfloat16), grow.astype(jnp.bfloat16), preferred_element_type=f32
    )
    for b in range(8):
        wx[b] = wide[:, blk(b)]
    place_tiles(own, near_f, far_f, packs, xt, xud, range(1, 9))
    dust_features(xt, xud, fe, INNER, ())

    def put_m(j, r, b, v):
        mm[j, r, b - 2] = v

    def put_z(j, r, b, re, im):
        zz[j - 1, 0, r, b - 2] = re
        zz[j - 1, 1, r, b - 2] = im

    pt = packs[:, blk(0)]
    zero = jnp.zeros((8, 128), f32)
    out = first_layer(
        fe, wx, INNER, (), put_m, None, put_z, (flag(pt, 0), flag(pt, 1)), [zero] * 3
    )
    for j in range(3):
        powers[j] = out[j]

    def put_energy(q, r, b, v):
        energies[r, b - 3] = v

    out = second_layer(
        0,
        CORE,
        lambda j, r, b: mm[j, r, b - 2],
        lambda j, ri, r, b, t: spread(zz, j - 1, ri, r, b - 2, t),
        wx,
        put_energy,
        [zero] * 16,
    )
    for k in range(16):
        sums[k] = out[k]


def outer_kernel(own, near_f, far_f, packs, near_p, far_p, mi, zi, wx, powers, sums, energies, stats, en0, en1, xt, xud, fe, mo, zo, sm, es, acc):
    f32 = jnp.float32
    place_tiles(own, near_f, far_f, packs, xt, xud, (1, 2, 7, 8))
    place_rims(packs, near_p, far_p, xt, xud)
    dust_features(xt, xud, fe, OUTER, ((10, 0), (11, 9)))

    def put_m(j, r, b, v):
        mo[j, r, EDGE[b]] = v

    def put_side(j, r, b, v):
        sm[j, b // 9, r] = v

    def put_z(j, r, b, re, im):
        zo[j - 1, 0, r, b // 8] = re
        zo[j - 1, 1, r, b // 8] = im

    pt = packs[:, blk(0)]
    f2, f3 = flag(pt, 2), flag(pt, 3)
    power = first_layer(
        fe,
        wx,
        OUTER,
        (0, 9),
        put_m,
        put_side,
        put_z,
        (flag(pt, 0), flag(pt, 1)),
        [powers[j] for j in range(3)],
    )
    for j in range(2):
        for r in range(8):
            mo[j, 4 + r, EDGE[0]] = jnp.where(f2, sm[j, 0, 7 - r], sm[j, 0, r])
            mo[j, 4 + r, EDGE[9]] = jnp.where(f3, sm[j, 1, 7 - r], sm[j, 1, r])

    def get_m(j, r, b):
        return mo[j, r, EDGE[b]] if b in EDGE else mi[j, r, b - 2]

    def get_z(j, ri, r, b, t):
        if b in EDGE:
            return spread(zo, j - 1, ri, r, b // 8, t)
        return spread(zi, j - 1, ri, r, b - 2, t)

    def put_energy(q, r, b, v):
        if q == 1:
            v = v + (energies[r, b - 3] if b in CORE else es[0, r, :, blk(b - 1)])
        es[q // 2, r, :, blk(b - 1)] = v

    zero = jnp.zeros((8, 128), f32)
    for q in range(3):
        blocks = (1, 2, 7, 8) if q == 0 else range(1, 9)
        start = [sums[k] for k in range(16)] if q == 0 else [zero] * 16
        out = second_layer(q, blocks, get_m, get_z, wx, put_energy, start)
        for k in range(16):
            kind, t = divmod(k, 8)
            acc[pl.ds(q * 128 + kind * 64 + t, 8, stride=8), :] = out[k]
    for r in range(8):
        en0[r : r + 1, :] = jnp.sum(es[0, r], axis=0, keepdims=True)
        en1[r : r + 1, :] = jnp.sum(es[1, r], axis=0, keepdims=True)
    lanes_summed = lax.dot_general(
        jnp.ones((8, 128), f32),
        acc[...],
        (((1,), (1,)), ((), ())),
        precision=lax.Precision.HIGHEST,
        preferred_element_type=f32,
    )
    w_sum = wx[0]
    for b in range(1, 8):
        w_sum = w_sum + wx[b]
    tail = jnp.zeros((1, 128), f32)
    for i, v in enumerate(power + [w_sum]):
        tail = jnp.where(lanes()[0:1] == i, jnp.sum(v), tail)
    for c in range(stats.shape[0]):
        for q in range(3):
            stats[c, q : q + 1, :] = lanes_summed[0:1, blk(q)]
        stats[c, 3:4, :] = tail


def middle_kernel(parts, out, *, n_y):
    x = lax.axis_index("x")
    total = parts[0]
    for i in range(1, parts.shape[0]):
        total = total + parts[i]
    mine = parts[x * n_y]
    for i in range(1, n_y):
        mine = mine + parts[x * n_y + i]
    for i in range(out.shape[0]):
        out[i, 0:4] = total
        out[i, 4:8] = mine


def final_kernel(parts, en0, en1, face_out, sky_out, energy, *, n_zl):
    first = (lax.axis_index("zh") * lax.axis_size("core") + lax.axis_index("core")) * n_zl
    total = parts[0, 0:4]
    for i in range(1, parts.shape[0]):
        total = total + parts[i, 0:4]
    mine = parts[first, 4:8]
    for i in range(1, n_zl):
        mine = mine + parts[first + i, 4:8]
    weight = total[3:4, 3:4]
    level = [total[3:4, j : j + 1] / (8.0 * weight) + EPS for j in range(3)]
    scale = [1.0 / jnp.sqrt(v) for v in level]
    lane = lax.broadcasted_iota(jnp.int32, (1, 128), 1)
    for q, (j1, j2) in enumerate(PAIRS):
        third = jnp.broadcast_to(scale[j1] * scale[j2], (1, 128))
        fourth = jnp.broadcast_to(1.0 / level[j1], (1, 128))
        factor = jnp.where(lane < 64, third, fourth)
        sky_out[q : q + 1, :] = total[q : q + 1] * (factor / weight)
        face_out[q, 0:1, :] = mine[q : q + 1] * (factor / mine[3:4, 3:4])
    a = jnp.broadcast_to(1.0 / (192.0 * level[0]), (8, 1024))
    b = jnp.broadcast_to(1.0 / (192.0 * level[1]), (8, 1024))
    energy[...] = en0[...] * a + en1[...] * b


def pair_exchange(value, axes):
    n = lax.axis_size(axes)
    far = lax.ppermute(value, axes, [(i, (i + (1 if i % 2 else n - 1)) % n) for i in range(n)])
    near = lax.ppermute(value, axes, [(i, i ^ 1) for i in range(n)])
    return near, far


def on_device(dust, seam_flags, block_weights):
    f32 = jnp.float32
    sds = jax.ShapeDtypeStruct
    vmem = pl.BlockSpec(memory_space=pltpu.VMEM)
    hbm = pl.BlockSpec(memory_space=pltpu.HBM)
    tile = pl.pallas_call(
        tile_kernel,
        out_shape=sds((8, 1152), f32),
        in_specs=[hbm, hbm],
        out_specs=vmem,
        scratch_shapes=[pltpu.SMEM((1, 1, 4), jnp.int32), pltpu.SemaphoreType.DMA((2,))],
        compiler_params=pltpu.CompilerParams(vmem_limit_bytes=2 << 20),
        name="tile_and_flags",
    )(*(pltpu.with_memory_space_constraint(v, pltpu.HBM) for v in (dust, seam_flags)))
    near_f, far_f = pair_exchange(tile, FACE)
    packs = pl.pallas_call(
        pack_kernel,
        out_shape=sds((8, 384), f32),
        in_specs=[vmem] * 3,
        out_specs=vmem,
        compiler_params=pltpu.CompilerParams(vmem_limit_bytes=2 << 20),
        name="edge_packs",
    )(tile, near_f, far_f)
    near_p, far_p = pair_exchange(packs, PATCH)
    inner = pl.pallas_call(
        inner_kernel,
        out_shape=(
            sds((2, 16, 6, 8, 128), f32),
            sds((2, 2, 8, 6, 8, 128), f32),
            sds((8, 8, 128), f32),
            sds((3, 8, 128), f32),
            sds((16, 8, 128), f32),
            sds((8, 4, 8, 128), f32),
        ),
        in_specs=[vmem] * 5,
        out_specs=(vmem,) * 6,
        scratch_shapes=[
            pltpu.VMEM((16, 1536), f32),
            pltpu.VMEM((16, 1536), f32),
            pltpu.VMEM((5, 8, 10, 8, 128), f32),
        ],
        compiler_params=pltpu.CompilerParams(vmem_limit_bytes=14 << 20),
        name="inner_columns",
    )(tile, near_f, far_f, packs, block_weights)
    n_y, n_zl = lax.axis_size("y"), lax.axis_size("zl")
    n_first, n_second = lax.axis_size(("x", "y")), lax.axis_size(("zh", "core", "zl"))
    stats, en0, en1 = pl.pallas_call(
        outer_kernel,
        out_shape=(sds((n_first, 4, 128), f32), sds((8, 1024), f32), sds((8, 1024), f32)),
        in_specs=[vmem] * 12,
        out_specs=(vmem,) * 3,
        scratch_shapes=[
            pltpu.VMEM((16, 1536), f32),
            pltpu.VMEM((16, 1536), f32),
            pltpu.VMEM((5, 8, 10, 8, 128), f32),
            pltpu.VMEM((2, 16, 4, 8, 128), f32),
            pltpu.VMEM((2, 2, 8, 2, 8, 128), f32),
            pltpu.VMEM((2, 2, 8, 8, 128), f32),
            pltpu.VMEM((2, 8, 8, 1024), f32),
            pltpu.VMEM((384, 128), f32),
        ],
        compiler_params=pltpu.CompilerParams(vmem_limit_bytes=14 << 20),
        name="both_layers",
    )(tile, near_f, far_f, packs, near_p, far_p, *inner)
    stats = lax.all_to_all(stats, ("x", "y"), 0, 0, tiled=True)
    stats = pl.pallas_call(
        lambda *refs: middle_kernel(*refs, n_y=n_y),
        out_shape=sds((n_second, 8, 128), f32),
        in_specs=[vmem],
        out_specs=vmem,
        compiler_params=pltpu.CompilerParams(vmem_limit_bytes=2 << 20),
        name="row_part",
    )(stats)
    stats = lax.all_to_all(stats, ("zh", "core", "zl"), 0, 0, tiled=True)
    face_moments, sky_moments, energy = pl.pallas_call(
        lambda *refs: final_kernel(*refs, n_zl=n_zl),
        out_shape=(sds((3, 1, 128), f32), sds((3, 128), f32), sds((8, 1024), f32)),
        in_specs=[vmem] * 3,
        out_specs=(vmem,) * 3,
        compiler_params=pltpu.CompilerParams(vmem_limit_bytes=2 << 20),
        name="finish",
    )(stats, en0, en1)
    return energy, jnp.swapaxes(face_moments, 0, 1), sky_moments


def solution(mesh):
    fine = Mesh(mesh.devices.reshape(4, 2, 2, 4, 8), FACE + PATCH)
    return jax.shard_map(
        on_device,
        mesh=fine,
        in_specs=(P(FACE, PATCH), P(FACE, PATCH, None), P(FACE, PATCH)),
        out_specs=(P(FACE, PATCH), P(FACE, None, None), P()),
        check_vma=False,
    )
```

```python
import math

import jax
import jax.numpy as jnp
import numpy as np
from jax import lax
from jax.experimental import pallas as pl
from jax.experimental.pallas import tpu as pltpu
from jax.sharding import Mesh
from jax.sharding import PartitionSpec as P

EPS = 1e-06
PAIRS = ((0, 1), (0, 2), (1, 2))
FACE = ("x", "zh", "core")
PATCH = ("zl", "y")
FLAG_LANE = 32


def filter_features():
    rows = np.repeat(np.array([-1.0, 0.0, 1.0]), 3)
    cols = np.tile(np.array([-1.0, 0.0, 1.0]), 3)
    env = np.exp(-(rows**2 + cols**2) / 1.28)
    at = {(int(a), int(b)): i for i, (a, b) in enumerate(zip(rows, cols))}
    picks = [at[0, 1], at[1, 0], at[1, 1], at[1, -1]]
    even, odd = [], []
    for t in range(8):
        h = math.pi * t / 8.0
        ph = 2.2 * (rows * math.cos(h) + cols * math.sin(h))
        c = np.cos(ph) - np.sum(env * np.cos(ph)) / np.sum(env)
        s = np.sin(ph) - np.sum(env * np.sin(ph)) / np.sum(env)
        norm = np.sqrt(np.sum(env**2 * (c**2 + s**2)))
        for src, dst in ((env * c / norm, even), (env * s / norm, odd)):
            v = src[picks]
            dst.append([v[0], v[1], (v[2] + v[3]) / 2, (v[2] - v[3]) / 2])
    out = np.array([even, odd])
    out[np.abs(out) < 1e-12] = 0.0
    return out


TABLE = filter_features()


def features(top, mid, bot, left, right):
    tl, tr = left(top), right(top)
    ml, mr = left(mid), right(mid)
    bl, br = left(bot), right(bot)
    top, mid, bot = (v[len(v) // 2] if isinstance(v, tuple) else v for v in (top, mid, bot))
    two = mid + mid
    s1, s2 = br + tl, bl + tr
    d1, d2 = br - tl, bl - tr
    return (
        ml + mr - two,
        top + bot - two,
        s1 + s2 - (two + two),
        s1 - s2,
        mr - ml,
        bot - top,
        d1 + d2,
        d1 - d2,
    )


def combos(ft):
    e01, e10, p, q, o01, o10, po, qo = ft

    def lin(pairs):
        total = None
        for c, v in pairs:
            if c == 0.0:
                continue
            term = float(c) * v
            total = term if total is None else total + term
        return total

    re, im = [None] * 8, [None] * 8
    for t in (0, 4):
        ce, co = TABLE[0, t], TABLE[1, t]
        re[t] = lin(zip(ce, (e01, e10, p, q)))
        im[t] = lin(zip(co, (o01, o10, po, qo)))
    for t in (1, 2, 3):
        ce, co = TABLE[0, t], TABLE[1, t]
        a, b = lin(zip(ce[:3], (e01, e10, p))), lin([(ce[3], q)])
        re[t], re[8 - t] = a + b, a - b
        a = lin([(co[0], o01), (co[3], qo)])
        b = lin([(co[1], o10), (co[2], po)])
        im[t], im[8 - t] = a + b, a - b
    return re, im


def tile_kernel(dust, flags, to_far, to_near, tile, pack, bits, sems):
    tile_copy = pltpu.make_async_copy(dust, tile, sems.at[0])
    flag_copy = pltpu.make_async_copy(flags, bits, sems.at[1])
    tile_copy.start()
    flag_copy.start()
    lane = lax.broadcasted_iota(jnp.int32, (8, 128), 1)
    row = jnp.zeros((8, 128), jnp.float32)
    flag_copy.wait()
    for i in range(4):
        row = jnp.where(lane == FLAG_LANE + i, bits[0, 0, i].astype(jnp.float32), row)
    tile_copy.wait()
    edges = jnp.where(lane < 64, tile[:, 0:128], tile[:, 896:1024])
    edges = jnp.where((lane < 16) | (lane >= 112), edges, row)
    pack[...] = edges
    to_near[48:56] = edges
    to_far[48:56] = edges
    odd = lax.axis_index("core") == 1
    for b in range(8):
        first, last = tile[0:6, blk(b)], tile[2:8, blk(b)]
        to_near[pl.ds(b, 6, stride=8), :] = jnp.where(odd, first, last)
        to_far[pl.ds(b, 6, stride=8), :] = jnp.where(odd, last, first)


def weight_kernel(bw, wx):
    grow = lax.broadcasted_iota(jnp.int32, (128, 1024), 1) // 8 == lax.broadcasted_iota(
        jnp.int32, (128, 1024), 0
    )
    wide = jnp.dot(
        bw[...].astype(jnp.bfloat16),
        grow.astype(jnp.bfloat16),
        preferred_element_type=jnp.float32,
    )
    for b in range(8):
        wx[b] = wide[:, blk(b)]


def sorted_pair(near, far, odd):
    return jnp.where(odd, near, far), jnp.where(odd, far, near)


def pack_kernel(pack, near, far, _, out):
    out[:, 0:128] = pack[...]
    a, b = sorted_pair(near[48:56], far[48:56], lax.axis_index("core") == 1)
    out[:, 128:256] = a
    out[:, 256:384] = b


def blk(b):
    return slice(128 * b, 128 * b + 128)


def lanes():
    return lax.broadcasted_iota(jnp.int32, (8, 128), 1)


def rows_of():
    return lax.broadcasted_iota(jnp.int32, (8, 128), 0)


def revl(v):
    return jnp.take_along_axis(v, 127 - lanes(), axis=1, mode="promise_in_bounds")


def revr(v):
    return jnp.take_along_axis(v, 7 - rows_of(), axis=0, mode="promise_in_bounds")


def flag(pack, i):
    return jnp.broadcast_to(pack[:, FLAG_LANE + i : FLAG_LANE + i + 1], (8, 128)) > 0.5


def spread(ref, *at):
    *lead, r = at
    return ref[(*lead, pl.ds(r, 8, stride=0), slice(None))]


def place_tiles(own, near_f, far_f, packs, xt, xud, blocks):
    odd_f = lax.axis_index("core") == 1
    pt, pu, pd = (packs[:, blk(i)] for i in range(3))
    f0, f1, f0d, f1u = flag(pt, 0), flag(pt, 1), flag(pd, 0), flag(pu, 1)

    def six_rows(b):
        rows = pl.ds(b, 6, stride=8)
        return sorted_pair(near_f[rows, :], far_f[rows, :], odd_f)

    def pad(v):
        return jnp.concatenate([v, v[0:2]], 0)

    for b in blocks:
        b, c = b - 1, 8 - b
        t_b, t_r = own[:, blk(b)], revl(own[:, blk(c)])
        u_b, d_b = six_rows(b)
        u_r, d_r = six_rows(c)
        xt[4:12, blk(b + 1)] = t_b
        xt[0:4, blk(b + 1)] = jnp.where(f0, revl(pad(u_r)), pad(u_b))[2:6]
        xt[12:16, blk(b + 1)] = jnp.where(f1, revl(pad(d_r)), pad(d_b))[0:4]
        xud[0:6, blk(b + 1)] = u_b
        xud[6:8, blk(b + 1)] = jnp.where(f1u, t_r, t_b)[0:2]
        xud[8:10, blk(b + 1)] = jnp.where(f0d, t_r, t_b)[6:8]
        xud[10:16, blk(b + 1)] = d_b


def place_rims(packs, near_p, far_p, xt, xud):
    low = lanes() < 64
    odd_p = lax.axis_index("y") % 2 == 1
    pt, pu, pd = (packs[:, blk(i)] for i in range(3))
    (plf, prt), (pul, pur), (pdl, pdr) = (
        sorted_pair(near_p[:, blk(i)], far_p[:, blk(i)], odd_p) for i in range(3)
    )
    w_ = jnp.where
    turn_t, turn_u, turn_d = revr(pt), revr(pu), revr(pd)
    revl_l, revl_r = revl(plf), revl(prt)
    xt[4:12, blk(0)] = w_(flag(pt, 2), revr(plf), plf)
    xt[0:4, blk(0)] = pul[4:8]
    xt[12:16, blk(0)] = pdl[0:4]
    xt[4:12, blk(9)] = w_(flag(pt, 3), revr(prt), prt)
    xt[0:4, blk(9)] = pur[4:8]
    xt[12:16, blk(9)] = pdr[0:4]
    xud[0:6, blk(0)] = w_(flag(pu, 2), revr(pul), pul)[2:8]
    xud[6:8, blk(0)] = plf[0:2]
    xud[8:10, blk(0)] = plf[6:8]
    xud[10:16, blk(0)] = w_(flag(pd, 2), revr(pdl), pdl)[0:6]
    xud[0:6, blk(9)] = w_(flag(pu, 3), revr(pur), pur)[2:8]
    xud[6:8, blk(9)] = prt[0:2]
    xud[8:10, blk(9)] = prt[6:8]
    xud[10:16, blk(9)] = w_(flag(pd, 3), revr(pdr), pdr)[0:6]
    xt[4:12, blk(10)] = w_(low, w_(flag(plf, 3), turn_t, pt), plf)
    xt[0:4, blk(10)] = w_(low, pu, w_(flag(plf, 0), revl(pul), pul))[4:8]
    xt[12:16, blk(10)] = w_(low, pd, w_(flag(plf, 1), revl(pdl), pdl))[0:4]
    xt[4:12, blk(11)] = w_(low, prt, w_(flag(prt, 2), turn_t, pt))
    xt[0:4, blk(11)] = w_(low, w_(flag(prt, 0), revl(pur), pur), pu)[4:8]
    xt[12:16, blk(11)] = w_(low, w_(flag(prt, 1), revl(pdr), pdr), pd)[0:4]
    xud[0:6, blk(10)] = w_(low, w_(flag(pul, 3), turn_u, pu), pul)[2:8]
    xud[6:8, blk(10)] = w_(low, pt, w_(flag(pul, 1), revl_l, plf))[0:2]
    xud[8:10, blk(10)] = w_(low, pt, w_(flag(pdl, 0), revl_l, plf))[6:8]
    xud[10:16, blk(10)] = w_(low, w_(flag(pdl, 3), turn_d, pd), pdl)[0:6]
    xud[0:6, blk(11)] = w_(low, pur, w_(flag(pur, 2), turn_u, pu))[2:8]
    xud[6:8, blk(11)] = w_(low, w_(flag(pur, 1), revl_r, prt), pt)[0:2]
    xud[8:10, blk(11)] = w_(low, w_(flag(pdr, 0), revl_r, prt), pt)[6:8]
    xud[10:16, blk(11)] = w_(low, pdr, w_(flag(pdr, 2), turn_d, pd))[0:6]


def dust_features(main, rims, fe, mains, sides):
    def load_own(s, b):
        xt, _ = main if 1 <= b <= 8 else rims
        return xt[4 + s : 12 + s, blk(b)]

    def load_ud(s, b):
        _, xud = main if 1 <= b <= 8 else rims
        return jnp.concatenate([xud[2 + s : 6 + s, blk(b)], xud[10 + s : 14 + s, blk(b)]], 0)

    for slot, load, d in ((0, load_own, 1), (1, load_own, 2), (2, load_own, 4), (3, load_ud, 1), (4, load_ud, 2)):
        left, right = shifts(d)
        for b in mains:
            rows = [tuple(load(s, c) for c in (b - 1, b, b + 1)) for s in (-d, 0, d)]
            for k, v in enumerate(features(*rows, left, right)):
                fe[slot, k, b] = v
        if d == 4:
            continue
        for b, dst in sides:
            rows = [load(s, b) for s in (-d, 0, d)]
            turn_l, turn_r = (lambda v: pltpu.roll(v, d, 1)), (lambda v: pltpu.roll(v, 128 - d, 1))
            for k, v in enumerate(features(*rows, turn_l, turn_r)):
                fe[slot, k, dst] = v


def shifts(d):
    lane = lanes()
    first, last = lane < d, lane >= 128 - d

    def left(v):
        return pltpu.roll(jnp.where(last, v[0], v[1]), d, 1)

    def right(v):
        return pltpu.roll(jnp.where(first, v[2], v[1]), 128 - d, 1)

    return left, right


def first_layer(fe, wx, blocks, sides, put_m, put_side, put_z, flips, start):
    sub = rows_of()

    def column(vals):
        out = jnp.full((8, 128), float(vals[0]), jnp.float32)
        for t in range(1, 8):
            out = jnp.where(sub == t, float(vals[t]), out)
        return out

    ce = [column(TABLE[0, :, k]) for k in range(4)]
    co = [column(TABLE[1, :, k]) for k in range(4)]

    def response(slot, r, b):
        v = [spread(fe, slot, k, b, r) for k in range(8)]
        re = ce[0] * v[0] + ce[1] * v[1] + (ce[2] * v[2] + ce[3] * v[3])
        im = co[0] * v[4] + co[1] * v[5] + (co[2] * v[6] + co[3] * v[7])
        return re, im, re * re + im * im

    powers = []
    for j in range(3):

        def row(r, total, j=j):
            for b in blocks:
                wr = spread(wx, b - 1, r)
                re, im, sq = response(j, r, b)
                total = total + wr * sq
                if j > 0:
                    put_z(j, r, b, wr * re, wr * im)
                if j < 2:
                    put_m(j, 4 + r, b, jnp.sqrt(sq + EPS))
            if j < 2:
                for b in sides:
                    put_side(j, r, b, jnp.sqrt(response(j, r, b)[2] + EPS))
            return total

        powers.append(lax.fori_loop(0, 8, row, start[j]))
    for j in range(2):

        def rim_row(i, _, j=j):
            for r, dst, f in ((i, i, flips[0]), (i + 4, i + 12, flips[1])):
                m = {b: jnp.sqrt(response(3 + j, r, b)[2] + EPS) for b in (*blocks, *sides)}
                for b in blocks:
                    put_m(j, dst, b, jnp.where(f, revl(m[9 - b]), m[b]))
                for b in sides:
                    put_m(j, dst, b, m[b])
            return 0

        lax.fori_loop(0, 4, rim_row, 0)
    return powers


def second_layer(q, blocks, get_m, get_z, wx, put_energy, start):
    j1, j2 = PAIRS[q]
    d = 2**j2
    left, right = shifts(d)

    def row(r, carry):
        carry = list(carry)
        for b in blocks:
            rows = [tuple(get_m(j1, r + (4 + s), c) for c in (b - 1, b, b + 1)) for s in (-d, 0, d)]
            re, im = combos(features(*rows, left, right))
            wr = spread(wx, b - 1, r)
            energy = None
            for t in range(8):
                carry[t] = carry[t] + (get_z(j2, 0, r, b, t) * re[t] + get_z(j2, 1, r, b, t) * im[t])
                sq = re[t] * re[t] + im[t] * im[t]
                carry[8 + t] = carry[8 + t] + wr * sq
                energy = sq if energy is None else energy + sq
            put_energy(q, r, b, energy)
        return tuple(carry)

    return lax.fori_loop(0, 8, row, tuple(start))


INNER = (2, 3, 4, 5, 6, 7)
OUTER = (1, 8)
CORE = (3, 4, 5, 6)
EDGE = {0: 0, 1: 1, 8: 2, 9: 3}


def inner_kernel(own, near_f, far_f, packs, wx, mm, zz, xt, xud, powers, sums, energies, fe):
    f32 = jnp.float32
    place_tiles(own, near_f, far_f, packs, xt, xud, range(1, 9))
    dust_features((xt, xud), None, fe, INNER, ())

    def put_m(j, r, b, v):
        mm[j, r, b - 2] = v

    def put_z(j, r, b, re, im):
        zz[j - 1, 0, r, b - 2] = re
        zz[j - 1, 1, r, b - 2] = im

    pt = packs[:, blk(0)]
    zero = jnp.zeros((8, 128), f32)
    out = first_layer(
        fe, wx, INNER, (), put_m, None, put_z, (flag(pt, 0), flag(pt, 1)), [zero] * 3
    )
    for j in range(3):
        powers[j] = out[j]

    def put_energy(q, r, b, v):
        energies[r, b - 3] = v

    out = second_layer(
        0,
        CORE,
        lambda j, r, b: mm[j, r, b - 2],
        lambda j, ri, r, b, t: spread(zz, j - 1, ri, r, b - 2, t),
        wx,
        put_energy,
        [zero] * 16,
    )
    for k in range(16):
        sums[k] = out[k]


def outer_kernel(packs, near_p, far_p, wx, mi, zi, xt, xud, powers, sums, energies, stats, en0, en1, xtr, xudr, fe, mo, zo, sm, es, acc):
    f32 = jnp.float32
    place_rims(packs, near_p, far_p, xtr, xudr)
    dust_features((xt, xud), (xtr, xudr), fe, OUTER, ((10, 0), (11, 9)))

    def put_m(j, r, b, v):
        mo[j, r, EDGE[b]] = v

    def put_side(j, r, b, v):
        sm[j, b // 9, r] = v

    def put_z(j, r, b, re, im):
        zo[j - 1, 0, r, b // 8] = re
        zo[j - 1, 1, r, b // 8] = im

    pt = packs[:, blk(0)]
    f2, f3 = flag(pt, 2), flag(pt, 3)
    power = first_layer(
        fe,
        wx,
        OUTER,
        (0, 9),
        put_m,
        put_side,
        put_z,
        (flag(pt, 0), flag(pt, 1)),
        [powers[j] for j in range(3)],
    )
    for j in range(2):
        for r in range(8):
            mo[j, 4 + r, EDGE[0]] = jnp.where(f2, sm[j, 0, 7 - r], sm[j, 0, r])
            mo[j, 4 + r, EDGE[9]] = jnp.where(f3, sm[j, 1, 7 - r], sm[j, 1, r])

    def get_m(j, r, b):
        return mo[j, r, EDGE[b]] if b in EDGE else mi[j, r, b - 2]

    def get_z(j, ri, r, b, t):
        if b in EDGE:
            return spread(zo, j - 1, ri, r, b // 8, t)
        return spread(zi, j - 1, ri, r, b - 2, t)

    def put_energy(q, r, b, v):
        if q == 1:
            v = v + (energies[r, b - 3] if b in CORE else es[0, r, :, blk(b - 1)])
        es[q // 2, r, :, blk(b - 1)] = v

    zero = jnp.zeros((8, 128), f32)
    for q in range(3):
        blocks = (1, 2, 7, 8) if q == 0 else range(1, 9)
        start = [sums[k] for k in range(16)] if q == 0 else [zero] * 16
        out = second_layer(q, blocks, get_m, get_z, wx, put_energy, start)
        for k in range(16):
            kind, t = divmod(k, 8)
            acc[pl.ds(q * 128 + kind * 64 + t, 8, stride=8), :] = out[k]
    for r in range(8):
        en0[r : r + 1, :] = jnp.sum(es[0, r], axis=0, keepdims=True)
        en1[r : r + 1, :] = jnp.sum(es[1, r], axis=0, keepdims=True)
    lanes_summed = lax.dot_general(
        jnp.ones((8, 128), f32),
        acc[...],
        (((1,), (1,)), ((), ())),
        precision=lax.Precision.HIGHEST,
        preferred_element_type=f32,
    )
    w_sum = wx[0]
    for b in range(1, 8):
        w_sum = w_sum + wx[b]
    tail = jnp.zeros((1, 128), f32)
    for i, v in enumerate(power + [w_sum]):
        tail = jnp.where(lanes()[0:1] == i, jnp.sum(v), tail)
    for c in range(stats.shape[0]):
        for q in range(3):
            stats[c, q : q + 1, :] = lanes_summed[0:1, blk(q)]
        stats[c, 3:4, :] = tail


def middle_kernel(parts, out, *, n_y):
    x = lax.axis_index("x")
    total = parts[0]
    for i in range(1, parts.shape[0]):
        total = total + parts[i]
    mine = parts[x * n_y]
    for i in range(1, n_y):
        mine = mine + parts[x * n_y + i]
    for i in range(out.shape[0]):
        out[i, 0:4] = total
        out[i, 4:8] = mine


def final_kernel(parts, en0, en1, face_out, sky_out, energy, *, n_zl):
    first = (lax.axis_index("zh") * lax.axis_size("core") + lax.axis_index("core")) * n_zl
    total = parts[0, 0:4]
    for i in range(1, parts.shape[0]):
        total = total + parts[i, 0:4]
    mine = parts[first, 4:8]
    for i in range(1, n_zl):
        mine = mine + parts[first + i, 4:8]
    weight = total[3:4, 3:4]
    level = [total[3:4, j : j + 1] / (8.0 * weight) + EPS for j in range(3)]
    scale = [1.0 / jnp.sqrt(v) for v in level]
    lane = lax.broadcasted_iota(jnp.int32, (1, 128), 1)
    for q, (j1, j2) in enumerate(PAIRS):
        third = jnp.broadcast_to(scale[j1] * scale[j2], (1, 128))
        fourth = jnp.broadcast_to(1.0 / level[j1], (1, 128))
        factor = jnp.where(lane < 64, third, fourth)
        sky_out[q : q + 1, :] = total[q : q + 1] * (factor / weight)
        face_out[q, 0:1, :] = mine[q : q + 1] * (factor / mine[3:4, 3:4])
    a = jnp.broadcast_to(1.0 / (192.0 * level[0]), (8, 1024))
    b = jnp.broadcast_to(1.0 / (192.0 * level[1]), (8, 1024))
    energy[...] = en0[...] * a + en1[...] * b


def pair_exchange(to_near, to_far, axes):
    n = lax.axis_size(axes)
    far = lax.ppermute(to_far, axes, [(i, (i + (1 if i % 2 else n - 1)) % n) for i in range(n)])
    near = lax.ppermute(to_near, axes, [(i, i ^ 1) for i in range(n)])
    return near, far


def on_device(dust, seam_flags, block_weights):
    f32 = jnp.float32
    sds = jax.ShapeDtypeStruct
    vmem = pl.BlockSpec(memory_space=pltpu.VMEM)
    hbm = pl.BlockSpec(memory_space=pltpu.HBM)
    to_far, to_near, tile, pack = pl.pallas_call(
        tile_kernel,
        out_shape=(sds((56, 128), f32), sds((56, 128), f32), sds((8, 1024), f32), sds((8, 128), f32)),
        in_specs=[hbm, hbm],
        out_specs=(vmem,) * 4,
        scratch_shapes=[pltpu.SMEM((1, 1, 4), jnp.int32), pltpu.SemaphoreType.DMA((2,))],
        compiler_params=pltpu.CompilerParams(vmem_limit_bytes=2 << 20),
        name="tile_and_flags",
    )(*(pltpu.with_memory_space_constraint(v, pltpu.HBM) for v in (dust, seam_flags)))
    near_f, far_f = pair_exchange(to_near, to_far, FACE)
    weights = pl.pallas_call(
        weight_kernel,
        out_shape=sds((8, 8, 128), f32),
        in_specs=[vmem],
        out_specs=vmem,
        compiler_params=pltpu.CompilerParams(vmem_limit_bytes=2 << 20),
        name="pixel_weights",
    )(block_weights)
    packs = pl.pallas_call(
        pack_kernel,
        out_shape=sds((8, 384), f32),
        in_specs=[vmem] * 4,
        out_specs=vmem,
        compiler_params=pltpu.CompilerParams(vmem_limit_bytes=2 << 20),
        name="edge_packs",
    )(pack, near_f, far_f, weights)
    near_p, far_p = pair_exchange(packs, packs, PATCH)
    inner = pl.pallas_call(
        inner_kernel,
        out_shape=(
            sds((2, 16, 6, 8, 128), f32),
            sds((2, 2, 8, 6, 8, 128), f32),
            sds((16, 1536), f32),
            sds((16, 1536), f32),
            sds((3, 8, 128), f32),
            sds((16, 8, 128), f32),
            sds((8, 4, 8, 128), f32),
        ),
        in_specs=[vmem] * 5,
        out_specs=(vmem,) * 7,
        scratch_shapes=[
            pltpu.VMEM((5, 8, 10, 8, 128), f32),
        ],
        compiler_params=pltpu.CompilerParams(vmem_limit_bytes=14 << 20),
        name="inner_columns",
    )(tile, near_f, far_f, packs, weights)
    n_y, n_zl = lax.axis_size("y"), lax.axis_size("zl")
    n_first, n_second = lax.axis_size(("x", "y")), lax.axis_size(("zh", "core", "zl"))
    stats, en0, en1 = pl.pallas_call(
        outer_kernel,
        out_shape=(sds((n_first, 4, 128), f32), sds((8, 1024), f32), sds((8, 1024), f32)),
        in_specs=[vmem] * 11,
        out_specs=(vmem,) * 3,
        scratch_shapes=[
            pltpu.VMEM((16, 1536), f32),
            pltpu.VMEM((16, 1536), f32),
            pltpu.VMEM((5, 8, 10, 8, 128), f32),
            pltpu.VMEM((2, 16, 4, 8, 128), f32),
            pltpu.VMEM((2, 2, 8, 2, 8, 128), f32),
            pltpu.VMEM((2, 2, 8, 8, 128), f32),
            pltpu.VMEM((2, 8, 8, 1024), f32),
            pltpu.VMEM((384, 128), f32),
        ],
        compiler_params=pltpu.CompilerParams(vmem_limit_bytes=14 << 20),
        name="both_layers",
    )(packs, near_p, far_p, weights, *inner)
    stats = lax.all_to_all(stats, ("x", "y"), 0, 0, tiled=True)
    stats = pl.pallas_call(
        lambda *refs: middle_kernel(*refs, n_y=n_y),
        out_shape=sds((n_second, 8, 128), f32),
        in_specs=[vmem],
        out_specs=vmem,
        compiler_params=pltpu.CompilerParams(vmem_limit_bytes=2 << 20),
        name="row_part",
    )(stats)
    stats = lax.all_to_all(stats, ("zh", "core", "zl"), 0, 0, tiled=True)
    face_moments, sky_moments, energy = pl.pallas_call(
        lambda *refs: final_kernel(*refs, n_zl=n_zl),
        out_shape=(sds((3, 1, 128), f32), sds((3, 128), f32), sds((8, 1024), f32)),
        in_specs=[vmem] * 3,
        out_specs=(vmem,) * 3,
        compiler_params=pltpu.CompilerParams(vmem_limit_bytes=2 << 20),
        name="finish",
    )(stats, en0, en1)
    return energy, jnp.swapaxes(face_moments, 0, 1), sky_moments


def solution(mesh):
    fine = Mesh(mesh.devices.reshape(4, 2, 2, 4, 8), FACE + PATCH)
    return jax.shard_map(
        on_device,
        mesh=fine,
        in_specs=(P(FACE, PATCH), P(FACE, PATCH, None), P(FACE, PATCH)),
        out_specs=(P(FACE, PATCH), P(FACE, None, None), P()),
        check_vma=False,
    )
```

```python
import math

import jax
import jax.numpy as jnp
import numpy as np
from jax import lax
from jax.experimental import pallas as pl
from jax.experimental.pallas import tpu as pltpu
from jax.sharding import Mesh
from jax.sharding import PartitionSpec as P

EPS = 1e-06
PAIRS = ((0, 1), (0, 2), (1, 2))
FACE = ("x", "zh", "core")
PATCH = ("zl", "y")
FLAG_LANE = 32


def filter_features():
    rows = np.repeat(np.array([-1.0, 0.0, 1.0]), 3)
    cols = np.tile(np.array([-1.0, 0.0, 1.0]), 3)
    env = np.exp(-(rows**2 + cols**2) / 1.28)
    at = {(int(a), int(b)): i for i, (a, b) in enumerate(zip(rows, cols))}
    picks = [at[0, 1], at[1, 0], at[1, 1], at[1, -1]]
    even, odd = [], []
    for t in range(8):
        h = math.pi * t / 8.0
        ph = 2.2 * (rows * math.cos(h) + cols * math.sin(h))
        c = np.cos(ph) - np.sum(env * np.cos(ph)) / np.sum(env)
        s = np.sin(ph) - np.sum(env * np.sin(ph)) / np.sum(env)
        norm = np.sqrt(np.sum(env**2 * (c**2 + s**2)))
        for src, dst in ((env * c / norm, even), (env * s / norm, odd)):
            v = src[picks]
            dst.append([v[0], v[1], (v[2] + v[3]) / 2, (v[2] - v[3]) / 2])
    out = np.array([even, odd])
    out[np.abs(out) < 1e-12] = 0.0
    return out


TABLE = filter_features()


def features(top, mid, bot, left, right):
    tl, tr = left(top), right(top)
    ml, mr = left(mid), right(mid)
    bl, br = left(bot), right(bot)
    top, mid, bot = (v[len(v) // 2] if isinstance(v, tuple) else v for v in (top, mid, bot))
    two = mid + mid
    s1, s2 = br + tl, bl + tr
    d1, d2 = br - tl, bl - tr
    return (
        ml + mr - two,
        top + bot - two,
        s1 + s2 - (two + two),
        s1 - s2,
        mr - ml,
        bot - top,
        d1 + d2,
        d1 - d2,
    )


def combos(ft):
    e01, e10, p, q, o01, o10, po, qo = ft

    def lin(pairs):
        total = None
        for c, v in pairs:
            if c == 0.0:
                continue
            term = float(c) * v
            total = term if total is None else total + term
        return total

    re, im = [None] * 8, [None] * 8
    for t in (0, 4):
        ce, co = TABLE[0, t], TABLE[1, t]
        re[t] = lin(zip(ce, (e01, e10, p, q)))
        im[t] = lin(zip(co, (o01, o10, po, qo)))
    for t in (1, 2, 3):
        ce, co = TABLE[0, t], TABLE[1, t]
        a, b = lin(zip(ce[:3], (e01, e10, p))), lin([(ce[3], q)])
        re[t], re[8 - t] = a + b, a - b
        a = lin([(co[0], o01), (co[3], qo)])
        b = lin([(co[1], o10), (co[2], po)])
        im[t], im[8 - t] = a + b, a - b
    return re, im


def tile_kernel(dust, flags, to_far, to_near, tile, pack, bits, sems):
    tile_copy = pltpu.make_async_copy(dust, tile, sems.at[0])
    flag_copy = pltpu.make_async_copy(flags, bits, sems.at[1])
    tile_copy.start()
    flag_copy.start()
    lane = lax.broadcasted_iota(jnp.int32, (8, 128), 1)
    row = jnp.zeros((8, 128), jnp.float32)
    flag_copy.wait()
    for i in range(4):
        row = jnp.where(lane == FLAG_LANE + i, bits[0, 0, i].astype(jnp.float32), row)
    tile_copy.wait()
    edges = jnp.where(lane < 64, tile[:, 0:128], tile[:, 896:1024])
    edges = jnp.where((lane < 16) | (lane >= 112), edges, row)
    pack[...] = edges
    to_near[48:56] = edges
    to_far[48:56] = edges
    odd = lax.axis_index("core") == 1
    for b in range(8):
        first, last = tile[0:6, blk(b)], tile[2:8, blk(b)]
        to_near[pl.ds(b, 6, stride=8), :] = jnp.where(odd, first, last)
        to_far[pl.ds(b, 6, stride=8), :] = jnp.where(odd, last, first)


def weight_kernel(bw, wx):
    grow = lax.broadcasted_iota(jnp.int32, (128, 1024), 1) // 8 == lax.broadcasted_iota(
        jnp.int32, (128, 1024), 0
    )
    wide = jnp.dot(
        bw[...].astype(jnp.bfloat16),
        grow.astype(jnp.bfloat16),
        preferred_element_type=jnp.float32,
    )
    for b in range(8):
        wx[b] = wide[:, blk(b)]


def sorted_pair(near, far, odd):
    return jnp.where(odd, near, far), jnp.where(odd, far, near)


def pack_kernel(pack, near, far, _, out):
    out[:, 0:128] = pack[...]
    a, b = sorted_pair(near[48:56], far[48:56], lax.axis_index("core") == 1)
    out[:, 128:256] = a
    out[:, 256:384] = b


def blk(b):
    return slice(128 * b, 128 * b + 128)


def lanes():
    return lax.broadcasted_iota(jnp.int32, (8, 128), 1)


def rows_of():
    return lax.broadcasted_iota(jnp.int32, (8, 128), 0)


def revl(v):
    return jnp.take_along_axis(v, 127 - lanes(), axis=1, mode="promise_in_bounds")


def revr(v):
    return jnp.take_along_axis(v, 7 - rows_of(), axis=0, mode="promise_in_bounds")


def flag(pack, i):
    return jnp.broadcast_to(pack[:, FLAG_LANE + i : FLAG_LANE + i + 1], (8, 128)) > 0.5


def spread(ref, *at):
    *lead, r = at
    return ref[(*lead, pl.ds(r, 8, stride=0), slice(None))]


def place_tiles(own, near_f, far_f, packs, xt, xud, blocks):
    odd_f = lax.axis_index("core") == 1
    pt, pu, pd = (packs[:, blk(i)] for i in range(3))
    f0, f1, f0d, f1u = flag(pt, 0), flag(pt, 1), flag(pd, 0), flag(pu, 1)

    def six_rows(b):
        rows = pl.ds(b, 6, stride=8)
        return sorted_pair(near_f[rows, :], far_f[rows, :], odd_f)

    def pad(v):
        return jnp.concatenate([v, v[0:2]], 0)

    for b in blocks:
        b, c = b - 1, 8 - b
        t_b, t_r = own[:, blk(b)], revl(own[:, blk(c)])
        u_b, d_b = six_rows(b)
        u_r, d_r = six_rows(c)
        xt[4:12, blk(b + 1)] = t_b
        xt[0:4, blk(b + 1)] = jnp.where(f0, revl(pad(u_r)), pad(u_b))[2:6]
        xt[12:16, blk(b + 1)] = jnp.where(f1, revl(pad(d_r)), pad(d_b))[0:4]
        xud[0:6, blk(b + 1)] = u_b
        xud[6:8, blk(b + 1)] = jnp.where(f1u, t_r, t_b)[0:2]
        xud[8:10, blk(b + 1)] = jnp.where(f0d, t_r, t_b)[6:8]
        xud[10:16, blk(b + 1)] = d_b


def place_rims(packs, near_p, far_p, xt, xud):
    low = lanes() < 64
    odd_p = lax.axis_index("y") % 2 == 1
    pt, pu, pd = (packs[:, blk(i)] for i in range(3))
    (plf, prt), (pul, pur), (pdl, pdr) = (
        sorted_pair(near_p[:, blk(i)], far_p[:, blk(i)], odd_p) for i in range(3)
    )
    w_ = jnp.where
    turn_t, turn_u, turn_d = revr(pt), revr(pu), revr(pd)
    revl_l, revl_r = revl(plf), revl(prt)
    xt[4:12, blk(0)] = w_(flag(pt, 2), revr(plf), plf)
    xt[0:4, blk(0)] = pul[4:8]
    xt[12:16, blk(0)] = pdl[0:4]
    xt[4:12, blk(9)] = w_(flag(pt, 3), revr(prt), prt)
    xt[0:4, blk(9)] = pur[4:8]
    xt[12:16, blk(9)] = pdr[0:4]
    xud[0:6, blk(0)] = w_(flag(pu, 2), revr(pul), pul)[2:8]
    xud[6:8, blk(0)] = plf[0:2]
    xud[8:10, blk(0)] = plf[6:8]
    xud[10:16, blk(0)] = w_(flag(pd, 2), revr(pdl), pdl)[0:6]
    xud[0:6, blk(9)] = w_(flag(pu, 3), revr(pur), pur)[2:8]
    xud[6:8, blk(9)] = prt[0:2]
    xud[8:10, blk(9)] = prt[6:8]
    xud[10:16, blk(9)] = w_(flag(pd, 3), revr(pdr), pdr)[0:6]
    xt[4:12, blk(10)] = w_(low, w_(flag(plf, 3), turn_t, pt), plf)
    xt[0:4, blk(10)] = w_(low, pu, w_(flag(plf, 0), revl(pul), pul))[4:8]
    xt[12:16, blk(10)] = w_(low, pd, w_(flag(plf, 1), revl(pdl), pdl))[0:4]
    xt[4:12, blk(11)] = w_(low, prt, w_(flag(prt, 2), turn_t, pt))
    xt[0:4, blk(11)] = w_(low, w_(flag(prt, 0), revl(pur), pur), pu)[4:8]
    xt[12:16, blk(11)] = w_(low, w_(flag(prt, 1), revl(pdr), pdr), pd)[0:4]
    xud[0:6, blk(10)] = w_(low, w_(flag(pul, 3), turn_u, pu), pul)[2:8]
    xud[6:8, blk(10)] = w_(low, pt, w_(flag(pul, 1), revl_l, plf))[0:2]
    xud[8:10, blk(10)] = w_(low, pt, w_(flag(pdl, 0), revl_l, plf))[6:8]
    xud[10:16, blk(10)] = w_(low, w_(flag(pdl, 3), turn_d, pd), pdl)[0:6]
    xud[0:6, blk(11)] = w_(low, pur, w_(flag(pur, 2), turn_u, pu))[2:8]
    xud[6:8, blk(11)] = w_(low, w_(flag(pur, 1), revl_r, prt), pt)[0:2]
    xud[8:10, blk(11)] = w_(low, w_(flag(pdr, 0), revl_r, prt), pt)[6:8]
    xud[10:16, blk(11)] = w_(low, pdr, w_(flag(pdr, 2), turn_d, pd))[0:6]


def dust_features(main, rims, fe, mains, sides):
    def load_own(s, b):
        xt, _ = main if 1 <= b <= 8 else rims
        return xt[4 + s : 12 + s, blk(b)]

    def load_ud(s, b):
        _, xud = main if 1 <= b <= 8 else rims
        return jnp.concatenate([xud[2 + s : 6 + s, blk(b)], xud[10 + s : 14 + s, blk(b)]], 0)

    for slot, load, d in ((0, load_own, 1), (1, load_own, 2), (2, load_own, 4), (3, load_ud, 1), (4, load_ud, 2)):
        left, right = shifts(d)
        for b in mains:
            rows = [tuple(load(s, c) for c in (b - 1, b, b + 1)) for s in (-d, 0, d)]
            for k, v in enumerate(features(*rows, left, right)):
                fe[slot, k, b] = v
        if d == 4:
            continue
        for b, dst in sides:
            rows = [load(s, b) for s in (-d, 0, d)]
            turn_l, turn_r = (lambda v: pltpu.roll(v, d, 1)), (lambda v: pltpu.roll(v, 128 - d, 1))
            for k, v in enumerate(features(*rows, turn_l, turn_r)):
                fe[slot, k, dst] = v


def shifts(d):
    lane = lanes()
    first, last = lane < d, lane >= 128 - d

    def left(v):
        return pltpu.roll(jnp.where(last, v[0], v[1]), d, 1)

    def right(v):
        return pltpu.roll(jnp.where(first, v[2], v[1]), 128 - d, 1)

    return left, right


def first_layer(fe, wx, blocks, sides, put_m, put_side, put_z, flips, start):
    sub = rows_of()

    def column(vals):
        out = jnp.full((8, 128), float(vals[0]), jnp.float32)
        for t in range(1, 8):
            out = jnp.where(sub == t, float(vals[t]), out)
        return out

    ce = [column(TABLE[0, :, k]) for k in range(4)]
    co = [column(TABLE[1, :, k]) for k in range(4)]

    def response(slot, r, b):
        v = [spread(fe, slot, k, b, r) for k in range(8)]
        re = ce[0] * v[0] + ce[1] * v[1] + (ce[2] * v[2] + ce[3] * v[3])
        im = co[0] * v[4] + co[1] * v[5] + (co[2] * v[6] + co[3] * v[7])
        return re, im, re * re + im * im

    powers = []
    for j in range(3):

        def row(r, total, j=j):
            for b in blocks:
                wr = spread(wx, b - 1, r)
                re, im, sq = response(j, r, b)
                total = total + wr * sq
                if j > 0:
                    put_z(j, r, b, wr * re, wr * im)
                if j < 2:
                    put_m(j, 4 + r, b, jnp.sqrt(sq + EPS))
            if j < 2:
                for b in sides:
                    put_side(j, r, b, jnp.sqrt(response(j, r, b)[2] + EPS))
            return total

        powers.append(lax.fori_loop(0, 8, row, start[j]))
    for j in range(2):

        def rim_row(i, _, j=j):
            for r, dst, f in ((i, i, flips[0]), (i + 4, i + 12, flips[1])):
                m = {b: jnp.sqrt(response(3 + j, r, b)[2] + EPS) for b in (*blocks, *sides)}
                for b in blocks:
                    put_m(j, dst, b, jnp.where(f, revl(m[9 - b]), m[b]))
                for b in sides:
                    put_m(j, dst, b, m[b])
            return 0

        lax.fori_loop(0, 4, rim_row, 0)
    return powers


def second_layer(q, blocks, get_m, get_z, wx, put_energy, start):
    j1, j2 = PAIRS[q]
    d = 2**j2
    left, right = shifts(d)

    def row(r, carry):
        carry = list(carry)
        for b in blocks:
            rows = [tuple(get_m(j1, r + (4 + s), c) for c in (b - 1, b, b + 1)) for s in (-d, 0, d)]
            re, im = combos(features(*rows, left, right))
            wr = spread(wx, b - 1, r)
            energy = None
            for t in range(8):
                carry[t] = carry[t] + (get_z(j2, 0, r, b, t) * re[t] + get_z(j2, 1, r, b, t) * im[t])
                sq = re[t] * re[t] + im[t] * im[t]
                carry[8 + t] = carry[8 + t] + wr * sq
                energy = sq if energy is None else energy + sq
            put_energy(q, r, b, energy)
        return tuple(carry)

    return lax.fori_loop(0, 8, row, tuple(start))


INNER = (2, 3, 4, 5, 6, 7)
OUTER = (1, 8)
CORE = (3, 4, 5, 6)
EDGE = {0: 0, 1: 1, 8: 2, 9: 3}


def sublane_sums(rows):
    sub = rows_of()
    for step in (4, 2, 1):
        keep = sub % (2 * step) < step
        merged = []
        for u, v in zip(rows[:step], rows[step:]):
            other = jnp.where(keep, v, u)
            if step == 4:
                other = pltpu.roll(other, 4, 0)
            else:
                other = jnp.where(
                    keep, pltpu.roll(other, 8 - step, 0), pltpu.roll(other, step, 0)
                )
            merged.append(jnp.where(keep, u, v) + other)
        rows = merged
    return rows[0]


def inner_kernel(own, near_f, far_f, packs, wx, mm, zz, xt, xud, powers, sums, energies, fe):
    f32 = jnp.float32
    place_tiles(own, near_f, far_f, packs, xt, xud, range(1, 9))
    dust_features((xt, xud), None, fe, INNER, ())

    def put_m(j, r, b, v):
        mm[j, r, b - 2] = v

    def put_z(j, r, b, re, im):
        zz[j - 1, 0, r, b - 2] = re
        zz[j - 1, 1, r, b - 2] = im

    pt = packs[:, blk(0)]
    zero = jnp.zeros((8, 128), f32)
    out = first_layer(
        fe, wx, INNER, (), put_m, None, put_z, (flag(pt, 0), flag(pt, 1)), [zero] * 3
    )
    for j in range(3):
        powers[j] = out[j]

    def put_energy(q, r, b, v):
        energies[r, b - 3] = v

    out = second_layer(
        0,
        CORE,
        lambda j, r, b: mm[j, r, b - 2],
        lambda j, ri, r, b, t: spread(zz, j - 1, ri, r, b - 2, t),
        wx,
        put_energy,
        [zero] * 16,
    )
    for k in range(16):
        sums[k] = out[k]


def outer_kernel(packs, near_p, far_p, wx, mi, zi, xt, xud, powers, sums, energies, stats, en0, en1, xtr, xudr, fe, mo, zo, sm, es, acc):
    f32 = jnp.float32
    place_rims(packs, near_p, far_p, xtr, xudr)
    dust_features((xt, xud), (xtr, xudr), fe, OUTER, ((10, 0), (11, 9)))

    def put_m(j, r, b, v):
        mo[j, r, EDGE[b]] = v

    def put_side(j, r, b, v):
        sm[j, b // 9, r] = v

    def put_z(j, r, b, re, im):
        zo[j - 1, 0, r, b // 8] = re
        zo[j - 1, 1, r, b // 8] = im

    pt = packs[:, blk(0)]
    f2, f3 = flag(pt, 2), flag(pt, 3)
    power = first_layer(
        fe,
        wx,
        OUTER,
        (0, 9),
        put_m,
        put_side,
        put_z,
        (flag(pt, 0), flag(pt, 1)),
        [powers[j] for j in range(3)],
    )
    for j in range(2):
        for r in range(8):
            mo[j, 4 + r, EDGE[0]] = jnp.where(f2, sm[j, 0, 7 - r], sm[j, 0, r])
            mo[j, 4 + r, EDGE[9]] = jnp.where(f3, sm[j, 1, 7 - r], sm[j, 1, r])

    def get_m(j, r, b):
        return mo[j, r, EDGE[b]] if b in EDGE else mi[j, r, b - 2]

    def get_z(j, ri, r, b, t):
        if b in EDGE:
            return spread(zo, j - 1, ri, r, b // 8, t)
        return spread(zi, j - 1, ri, r, b - 2, t)

    def put_energy(q, r, b, v):
        if q == 1:
            v = v + (energies[r, b - 3] if b in CORE else es[0, r, :, blk(b - 1)])
        es[q // 2, r, :, blk(b - 1)] = v

    zero = jnp.zeros((8, 128), f32)
    for q in range(3):
        blocks = (1, 2, 7, 8) if q == 0 else range(1, 9)
        start = [sums[k] for k in range(16)] if q == 0 else [zero] * 16
        out = second_layer(q, blocks, get_m, get_z, wx, put_energy, start)
        for k in range(16):
            kind, t = divmod(k, 8)
            acc[pl.ds(q * 128 + kind * 64 + t, 8, stride=8), :] = out[k]
    for plane, out_ref in ((0, en0), (1, en1)):
        for b in range(8):
            out_ref[:, blk(b)] = sublane_sums([es[plane, r, :, blk(b)] for r in range(8)])
    lanes_summed = lax.dot_general(
        jnp.ones((8, 128), f32),
        acc[...],
        (((1,), (1,)), ((), ())),
        precision=lax.Precision.HIGHEST,
        preferred_element_type=f32,
    )
    w_sum = wx[0]
    for b in range(1, 8):
        w_sum = w_sum + wx[b]
    tail = jnp.zeros((1, 128), f32)
    for i, v in enumerate(power + [w_sum]):
        tail = jnp.where(lanes()[0:1] == i, jnp.sum(v), tail)
    for c in range(stats.shape[0]):
        for q in range(3):
            stats[c, q : q + 1, :] = lanes_summed[0:1, blk(q)]
        stats[c, 3:4, :] = tail


def middle_kernel(parts, out, *, n_y):
    x = lax.axis_index("x")
    total = parts[0]
    for i in range(1, parts.shape[0]):
        total = total + parts[i]
    mine = parts[x * n_y]
    for i in range(1, n_y):
        mine = mine + parts[x * n_y + i]
    for i in range(out.shape[0]):
        out[i, 0:4] = total
        out[i, 4:8] = mine


def final_kernel(parts, en0, en1, face_out, sky_out, energy, *, n_zl):
    first = (lax.axis_index("zh") * lax.axis_size("core") + lax.axis_index("core")) * n_zl
    total = parts[0, 0:4]
    for i in range(1, parts.shape[0]):
        total = total + parts[i, 0:4]
    mine = parts[first, 4:8]
    for i in range(1, n_zl):
        mine = mine + parts[first + i, 4:8]
    weight = total[3:4, 3:4]
    level = [total[3:4, j : j + 1] / (8.0 * weight) + EPS for j in range(3)]
    scale = [1.0 / jnp.sqrt(v) for v in level]
    lane = lax.broadcasted_iota(jnp.int32, (1, 128), 1)
    for q, (j1, j2) in enumerate(PAIRS):
        third = jnp.broadcast_to(scale[j1] * scale[j2], (1, 128))
        fourth = jnp.broadcast_to(1.0 / level[j1], (1, 128))
        factor = jnp.where(lane < 64, third, fourth)
        sky_out[q : q + 1, :] = total[q : q + 1] * (factor / weight)
        face_out[q, 0:1, :] = mine[q : q + 1] * (factor / mine[3:4, 3:4])
    a = jnp.broadcast_to(1.0 / (192.0 * level[0]), (8, 1024))
    b = jnp.broadcast_to(1.0 / (192.0 * level[1]), (8, 1024))
    energy[...] = en0[...] * a + en1[...] * b


def pair_exchange(to_near, to_far, axes):
    n = lax.axis_size(axes)
    far = lax.ppermute(to_far, axes, [(i, (i + (1 if i % 2 else n - 1)) % n) for i in range(n)])
    near = lax.ppermute(to_near, axes, [(i, i ^ 1) for i in range(n)])
    return near, far


def on_device(dust, seam_flags, block_weights):
    f32 = jnp.float32
    sds = jax.ShapeDtypeStruct
    vmem = pl.BlockSpec(memory_space=pltpu.VMEM)
    hbm = pl.BlockSpec(memory_space=pltpu.HBM)
    to_far, to_near, tile, pack = pl.pallas_call(
        tile_kernel,
        out_shape=(sds((56, 128), f32), sds((56, 128), f32), sds((8, 1024), f32), sds((8, 128), f32)),
        in_specs=[hbm, hbm],
        out_specs=(vmem,) * 4,
        scratch_shapes=[pltpu.SMEM((1, 1, 4), jnp.int32), pltpu.SemaphoreType.DMA((2,))],
        compiler_params=pltpu.CompilerParams(vmem_limit_bytes=2 << 20),
        name="tile_and_flags",
    )(*(pltpu.with_memory_space_constraint(v, pltpu.HBM) for v in (dust, seam_flags)))
    near_f, far_f = pair_exchange(to_near, to_far, FACE)
    weights = pl.pallas_call(
        weight_kernel,
        out_shape=sds((8, 8, 128), f32),
        in_specs=[vmem],
        out_specs=vmem,
        compiler_params=pltpu.CompilerParams(vmem_limit_bytes=2 << 20),
        name="pixel_weights",
    )(block_weights)
    packs = pl.pallas_call(
        pack_kernel,
        out_shape=sds((8, 384), f32),
        in_specs=[vmem] * 4,
        out_specs=vmem,
        compiler_params=pltpu.CompilerParams(vmem_limit_bytes=2 << 20),
        name="edge_packs",
    )(pack, near_f, far_f, weights)
    near_p, far_p = pair_exchange(packs, packs, PATCH)
    inner = pl.pallas_call(
        inner_kernel,
        out_shape=(
            sds((2, 16, 6, 8, 128), f32),
            sds((2, 2, 8, 6, 8, 128), f32),
            sds((16, 1536), f32),
            sds((16, 1536), f32),
            sds((3, 8, 128), f32),
            sds((16, 8, 128), f32),
            sds((8, 4, 8, 128), f32),
        ),
        in_specs=[vmem] * 5,
        out_specs=(vmem,) * 7,
        scratch_shapes=[
            pltpu.VMEM((5, 8, 10, 8, 128), f32),
        ],
        compiler_params=pltpu.CompilerParams(vmem_limit_bytes=14 << 20),
        name="inner_columns",
    )(tile, near_f, far_f, packs, weights)
    n_y, n_zl = lax.axis_size("y"), lax.axis_size("zl")
    n_first, n_second = lax.axis_size(("x", "y")), lax.axis_size(("zh", "core", "zl"))
    stats, en0, en1 = pl.pallas_call(
        outer_kernel,
        out_shape=(sds((n_first, 4, 128), f32), sds((8, 1024), f32), sds((8, 1024), f32)),
        in_specs=[vmem] * 11,
        out_specs=(vmem,) * 3,
        scratch_shapes=[
            pltpu.VMEM((16, 1536), f32),
            pltpu.VMEM((16, 1536), f32),
            pltpu.VMEM((5, 8, 10, 8, 128), f32),
            pltpu.VMEM((2, 16, 4, 8, 128), f32),
            pltpu.VMEM((2, 2, 8, 2, 8, 128), f32),
            pltpu.VMEM((2, 2, 8, 8, 128), f32),
            pltpu.VMEM((2, 8, 8, 1024), f32),
            pltpu.VMEM((384, 128), f32),
        ],
        compiler_params=pltpu.CompilerParams(vmem_limit_bytes=14 << 20),
        name="both_layers",
    )(packs, near_p, far_p, weights, *inner)
    stats = lax.all_to_all(stats, ("x", "y"), 0, 0, tiled=True)
    stats = pl.pallas_call(
        lambda *refs: middle_kernel(*refs, n_y=n_y),
        out_shape=sds((n_second, 8, 128), f32),
        in_specs=[vmem],
        out_specs=vmem,
        compiler_params=pltpu.CompilerParams(vmem_limit_bytes=2 << 20),
        name="row_part",
    )(stats)
    stats = lax.all_to_all(stats, ("zh", "core", "zl"), 0, 0, tiled=True)
    face_moments, sky_moments, energy = pl.pallas_call(
        lambda *refs: final_kernel(*refs, n_zl=n_zl),
        out_shape=(sds((3, 1, 128), f32), sds((3, 128), f32), sds((8, 1024), f32)),
        in_specs=[vmem] * 3,
        out_specs=(vmem,) * 3,
        compiler_params=pltpu.CompilerParams(vmem_limit_bytes=2 << 20),
        name="finish",
    )(stats, en0, en1)
    return energy, jnp.swapaxes(face_moments, 0, 1), sky_moments


def solution(mesh):
    fine = Mesh(mesh.devices.reshape(4, 2, 2, 4, 8), FACE + PATCH)
    return jax.shard_map(
        on_device,
        mesh=fine,
        in_specs=(P(FACE, PATCH), P(FACE, PATCH, None), P(FACE, PATCH)),
        out_specs=(P(FACE, PATCH), P(FACE, None, None), P()),
        check_vma=False,
    )
```
